32 devices in a mesh: seq: 8 (over y, x, core), mp: 4 (over z).
Axes of the slice: x: 2, y: 2, z: 4, core: 2. Of those that a mesh axis runs over, the one named last changes fastest.
Arguments:
- vit_hidden: bfloat16 [2048, 3200], P('seq'), may hold values from -6 to 6
- vit_gain: float32 [3200], replicated, may hold values from 0.5 to 1.5
- vit_bias: float32 [3200], replicated, may hold values from -3 to 3
- proj_weight: bfloat16 [3200, 8192], P(None, 'mp'), may hold values from -0.109375 to 0.109375
- text_emb: bfloat16 [4096, 8192], P('seq', 'mp'), may hold values from -40 to 40
- llm_gain: float32 [8192], P('mp'), may hold values from 0.5 to 1.5
- cotangent: bfloat16 [4096, 8192], P('seq', 'mp'), may hold values from -6 to 6
- tile_start: int32 [8], replicated, may hold values from 0 to 480, as said below
- tile_owner: int32 [8], replicated, may hold values from 0 to 7, each once
Outputs:
- normed: bfloat16 [4096, 8192], P('seq', 'mp')
- grad_text: bfloat16 [4096, 8192], P('seq', 'mp')
- grad_vit: bfloat16 [2048, 3200], P('seq', 'mp')
The draws below stay inside these ranges and needn't reach their ends.
Inputs may be any that keep to these rules, and one draw needn't show every extreme that they name: `tile_start`: starts increase with the tile's index and tiles never intersect; tile 0 begins the packed stretch and the last tile ends it.
All inputs are finite; a program needn't handle non-finite values.
Results may differ from the reference program's by a relative error of at most 0.0015.
The reference program's roundings to bfloat16 on the way (of `normed_vit`, `image_embed`, `merged` and `grad_embed`) count: a program that leaves them out, or rounds other values in their place, can miss the bound.
Values may be sent and summed in bfloat16 or wider, within the bound.
No kernel may reach another device: no remote copies, remote signals or barrier semaphores. Data moves between devices by JAX's collectives and lax.ppermute only.
A program may use at most 64 MiB of HBM per device.

```python
import jax
import jax.numpy as jnp
from jax import lax

D = 8192
DV = 3200
BLK = 8
TILE_BLOCKS = 32
LOCAL_BLOCKS = 64
TILES = 8
VROWS = 2048
TOKENS = 4096
SEQ_BLOCKS = 512
TEXT_BLOCKS = 256


def draw_text_emb(key, part):
    base_key = jax.random.fold_in(key, 11)
    first_key, second_key, third_key = jax.random.split(base_key, 3)
    columns = jnp.arange(D, dtype=jnp.float32) / D
    column_scale = 0.3 * jnp.exp(columns * jnp.log(3.0)) * jnp.exp(jax.random.uniform(second_key, (D,), jnp.float32, 0.0, jnp.log(3.0)))
    row_scale = jnp.exp(jax.random.uniform(third_key, (TOKENS, 1), jnp.float32, jnp.log(0.35), jnp.log(3.5)))
    base = jnp.clip(jax.random.normal(first_key, (TOKENS, D), jnp.float32), -4.0, 4.0)
    return (base * column_scale * row_scale).astype(jnp.bfloat16)


def draw_tile_start(key, part):
    gap_key = jax.random.fold_in(key, 23)
    gaps = jax.random.randint(gap_key, (TILES,), 0, TEXT_BLOCKS + 1)
    gaps = jnp.sort(gaps)
    gaps = gaps.at[0].set(0).at[TILES - 1].set(TEXT_BLOCKS)
    return (gaps + TILE_BLOCKS * jnp.arange(TILES)).astype(jnp.int32)


def shard_levels(rng, extent, cuts, smallest, high):
    def one(dim, shards_of):
        heights = jax.random.uniform(jax.random.fold_in(jax.random.fold_in(rng, 6), dim), (shards_of,), jnp.float32, smallest / len(cuts), high / len(cuts))
        return jnp.repeat(jnp.exp(heights), extent[dim] // shards_of).reshape((-1,) + (1,) * (len(extent) - dim - 1))

    level = one(*cuts[0])
    for cut in cuts[1:]:
        level = level * one(*cut)
    return level


def bell_draw(own_key, extent, scale, most, cuts=(), kind=jnp.bfloat16):
    array = scale * jax.random.normal(own_key, extent, jnp.float32)
    if cuts:
        array = array * shard_levels(own_key, extent, cuts, -0.22, 0.18)
    return jnp.clip(array, -most, most).astype(kind)


def setup_inputs(seed: int = 0) -> dict:
    arg_keys = jax.random.split(jax.random.key(seed), 10)
    vit_hidden = bell_draw(arg_keys[0], (VROWS, DV), 1.0, 6.0, ((0, 8),))
    vit_gain = jnp.clip(1.0 + 0.1 * jax.random.normal(arg_keys[1], (DV,), jnp.float32), 0.5, 1.5)
    vit_bias = bell_draw(arg_keys[2], (DV,), 0.5, 3.0, (), jnp.float32)
    proj_weight = bell_draw(arg_keys[3], (DV, D), DV ** -0.5, 0.109375, ((1, 4),))
    text_emb = draw_text_emb(jax.random.fold_in(arg_keys[9], 71), 0)
    llm_gain = jnp.clip(1.0 + 0.1 * jax.random.normal(arg_keys[5], (D,), jnp.float32), 0.5, 1.5)
    cotangent = bell_draw(arg_keys[6], (TOKENS, D), 1.0, 6.0, ((0, 8), (1, 4)))
    tile_start = draw_tile_start(jax.random.fold_in(arg_keys[9], 71), 0)
    tile_owner = jax.random.permutation(arg_keys[8], TILES).astype(jnp.int32)
    return {"vit_hidden": vit_hidden, "vit_gain": vit_gain, "vit_bias": vit_bias, "proj_weight": proj_weight, "text_emb": text_emb, "llm_gain": llm_gain, "cotangent": cotangent, "tile_start": tile_start, "tile_owner": tile_owner}


EPSILON = 1e-05

def reference(vit_hidden, vit_gain, vit_bias, proj_weight, text_emb, llm_gain, cotangent, tile_start, tile_owner):
    values = vit_hidden.astype(jnp.float32)
    centred = values - lax.optimization_barrier(jnp.mean(values, axis=1, keepdims=True))
    inv_std = lax.rsqrt(lax.optimization_barrier(jnp.mean(centred * centred, axis=1, keepdims=True)) + EPSILON)
    unit_rows = centred * inv_std
    normed_vit = (unit_rows * vit_gain + vit_bias).astype(jnp.bfloat16)
    image_embed = jnp.dot(normed_vit, proj_weight, preferred_element_type=jnp.float32).astype(jnp.bfloat16)
    row_block = jnp.arange(SEQ_BLOCKS, dtype=jnp.int32)
    global_block = (row_block % LOCAL_BLOCKS * TILES + row_block // LOCAL_BLOCKS).astype(jnp.int32)
    started = (tile_start[None, :] <= global_block[:, None]).astype(jnp.int32)
    found = (lax.optimization_barrier(jnp.sum(started, axis=1)) - 1).astype(jnp.int32)
    tile_index = jnp.maximum(found, 0).astype(jnp.int32)
    offset = (global_block - jnp.take(tile_start, tile_index)).astype(jnp.int32)
    inside = (found >= 0) & (offset < TILE_BLOCKS)
    source = jnp.where(inside, jnp.take(tile_owner, tile_index) * TILE_BLOCKS + offset, 0).astype(jnp.int32)
    embed_blocks = image_embed.reshape(TILES * TILE_BLOCKS, BLK, D)
    text_blocks = text_emb.reshape(SEQ_BLOCKS, BLK, D)
    merged = jnp.where(inside[:, None, None], jnp.take(embed_blocks, source, axis=0), text_blocks).reshape(TOKENS, D)
    merged_f = merged.astype(jnp.float32)
    grad_gain = llm_gain * cotangent.astype(jnp.float32)
    squares = lax.optimization_barrier(jnp.sum(merged_f * merged_f, axis=1))
    products = lax.optimization_barrier(jnp.sum(grad_gain * merged_f, axis=1))
    inv_rms = lax.rsqrt(squares / D + EPSILON)
    normed = (merged_f * inv_rms[:, None] * llm_gain).astype(jnp.bfloat16)
    grad_merged = inv_rms[:, None] * grad_gain - merged_f * (inv_rms * inv_rms * inv_rms * products / D)[:, None]
    image_rows = jnp.repeat(inside, BLK)
    grad_text = jnp.where(image_rows[:, None], 0.0, grad_merged).astype(jnp.bfloat16)
    grad_blocks = grad_merged.astype(jnp.bfloat16).reshape(SEQ_BLOCKS, BLK, D)
    target = jnp.where(inside, source, TILES * TILE_BLOCKS).astype(jnp.int32)
    grad_embed = jnp.zeros((TILES * TILE_BLOCKS, BLK, D), jnp.bfloat16).at[target].set(grad_blocks, mode='drop').reshape(VROWS, D)
    grad_normed = jnp.dot(grad_embed, proj_weight.T, preferred_element_type=jnp.float32)
    scaled = grad_normed * vit_gain
    first = lax.optimization_barrier(jnp.mean(scaled, axis=1, keepdims=True))
    second = lax.optimization_barrier(jnp.mean(scaled * unit_rows, axis=1, keepdims=True))
    grad_vit = (inv_std * (scaled - first - unit_rows * second)).astype(jnp.bfloat16)
    return (normed, grad_text, grad_vit)
```

```python
import functools

import jax
import jax.numpy as jnp
from jax import lax
from jax.experimental import pallas as pl
from jax.experimental.pallas import tpu as pltpu
from jax.sharding import PartitionSpec as P

D = 8192
DV = 3200
BLK = 8
TILE_BLOCKS = 32
ROWS = TILE_BLOCKS * BLK
EPSILON = 1e-05
LANES = 128
HEAD = 16
FULL = 32767.0
STEPS_PER_OCTAVE = 16.0
LN2 = 0.6931471805599453
F32 = jnp.float32
BF16 = jnp.bfloat16
I32 = jnp.int32
I16 = jnp.int16


def struct(shape, kind):
    return jax.ShapeDtypeStruct(shape, kind)


def smem():
    return pl.BlockSpec(memory_space=pltpu.SMEM)


def params(mib):
    return pltpu.CompilerParams(vmem_limit_bytes=mib << 20)


def cost(flops, moved):
    return pl.CostEstimate(flops=int(flops), bytes_accessed=int(moved), transcendentals=0)


def column(row):
    return jnp.transpose(jnp.broadcast_to(row, (LANES, row.shape[1])))


def as_row(col):
    return jnp.transpose(jnp.broadcast_to(col, (col.shape[0], LANES)))


def own_start_of(own, starts, owners, tiles):
    found = starts[0]
    for t in range(1, tiles):
        found = jnp.where(owners[t] == own, starts[t], found)
    return found


def norm_stats(values):
    mean = jnp.mean(values, axis=1, keepdims=True)
    centred = values - mean
    inv_std = lax.rsqrt(jnp.mean(centred * centred, axis=1, keepdims=True) + EPSILON)
    return mean, centred, inv_std


def embed_kernel(ranks, slots, tiles, own, starts, owners, x, vg, vb, w, out, natural, ordered):
    @pl.when(pl.program_id(0) == 0)
    def _():
        start = own_start_of(own[0], starts, owners, tiles)
        for c in range(0, ROWS, 64):
            _, centred, inv_std = norm_stats(x[c : c + 64, :].astype(F32))
            normed = (centred * inv_std * vg[...] + vb[...]).astype(BF16)
            natural[c : c + 64, :] = normed.astype(F32)
        for p in range(0, ranks * slots, 2):
            pair = []
            for q in (p, p + 1):
                block = lax.rem(q // slots - start + ranks * 1024, ranks) + (q % slots) * ranks
                block = jnp.minimum(block, TILE_BLOCKS - 1)
                pair.append(natural[pl.ds(pl.multiple_of(block * BLK, BLK), BLK), :])
            ordered[p * BLK : (p + 2) * BLK, :] = jnp.concatenate(pair, axis=0).astype(BF16)

    out[...] = jnp.dot(ordered[...], w[...], preferred_element_type=F32).astype(BF16)


def embed(own, starts, owners, x, vg, vb, w, ranks, slots):
    width = w.shape[1]
    tile = min(256, width)
    rows = ranks * slots * BLK
    whole = lambda i: (0, 0)
    return pl.pallas_call(
        functools.partial(embed_kernel, ranks, slots, starts.shape[0]),
        grid=(width // tile,),
        in_specs=[
            smem(),
            smem(),
            smem(),
            pl.BlockSpec((ROWS, DV), whole),
            pl.BlockSpec((1, DV), whole),
            pl.BlockSpec((1, DV), whole),
            pl.BlockSpec((DV, tile), lambda i: (0, i)),
        ],
        out_specs=pl.BlockSpec((rows, tile), lambda i: (0, i)),
        out_shape=struct((rows, width), BF16),
        scratch_shapes=[pltpu.VMEM((ROWS, DV), F32), pltpu.VMEM((rows, DV), BF16)],
        compiler_params=params(40),
        cost_estimate=cost(2 * rows * DV * width, 2 * DV * width + 4 * ROWS * DV),
        name="embed",
    )(own, starts, owners, x, vg, vb, w)


def units_kernel(x, vg, units, gains, inv):
    mean, _, inv_std = norm_stats(x[...].astype(F32))
    inv[...] = as_row(inv_std)[:BLK, :]
    for c in range(0, DV, 640):
        part = (x[:, c : c + 640].astype(F32) - mean) * inv_std
        units[c : c + 640, :] = jnp.transpose(part)
        gains[c : c + 640, :] = column(vg[:, c : c + 640])


def units_of(x, vg):
    return pl.pallas_call(
        units_kernel,
        out_shape=(struct((DV, ROWS), F32), struct((DV, LANES), F32), struct((BLK, ROWS), F32)),
        compiler_params=params(40),
        cost_estimate=cost(10 * ROWS * DV, 8 * ROWS * DV),
        name="units",
    )(x, vg)


def sums_of(m, gc):
    squares = as_row(jnp.sum(m * m, axis=1, keepdims=True))[:BLK, :]
    products = as_row(jnp.sum(gc * m, axis=1, keepdims=True))[:BLK, :]
    first = lax.broadcasted_iota(I32, squares.shape, 0) == 0
    return jnp.where(first, squares, products)


def text_sums_kernel(text, cot, gain, out):
    out[...] = sums_of(text[...].astype(F32), gain[...] * cot[...].astype(F32))


def text_sums(text, cot, gain):
    rows, width = text.shape
    step = lambda i: (i, 0)
    return pl.pallas_call(
        text_sums_kernel,
        grid=(rows // LANES,),
        in_specs=[
            pl.BlockSpec((LANES, width), step),
            pl.BlockSpec((LANES, width), step),
            pl.BlockSpec((1, width), lambda i: (0, 0)),
        ],
        out_specs=pl.BlockSpec((BLK, LANES), lambda i: (0, i)),
        out_shape=struct((BLK, rows), F32),
        compiler_params=params(24),
        cost_estimate=cost(6 * rows * width, 4 * rows * width),
        name="text_sums",
    )(text, cot, gain)


def image_sums_kernel(image, m, cot, gain, text, out):
    i = pl.program_id(0)

    @pl.when(i == 0)
    def _():
        out[:, image:] = text[...]

    found = sums_of(m[...].astype(F32), gain[...] * cot[...].astype(F32))
    out[:, pl.ds(pl.multiple_of(i * LANES, LANES), LANES)] = found


def image_sums(m, cot, gain, text):
    rows, width = m.shape
    total = rows + text.shape[1]
    step = lambda i: (i, 0)
    whole = lambda i: (0, 0)
    return pl.pallas_call(
        functools.partial(image_sums_kernel, rows),
        grid=(rows // LANES,),
        in_specs=[
            pl.BlockSpec((LANES, width), step),
            pl.BlockSpec((LANES, width), step),
            pl.BlockSpec((1, width), whole),
            pl.BlockSpec((BLK, text.shape[1]), whole),
        ],
        out_specs=pl.BlockSpec((BLK, total), whole),
        out_shape=struct((BLK, total), F32),
        compiler_params=params(24),
        cost_estimate=cost(6 * rows * width, 4 * rows * width),
        name="image_sums",
    )(m, cot, gain, text)


def row_factors(sums):
    inv_rms = lax.rsqrt(sums[0:1, :] / D + EPSILON)
    return inv_rms, inv_rms * inv_rms * inv_rms * sums[1:2, :] / D


def image_grad_kernel(m, cot, gain, sums, out):
    inv_rms, factor = row_factors(sums[...])
    inv_rms, factor = column(inv_rms)[:, :1], column(factor)[:, :1]
    grad_gain = gain[...] * cot[...].astype(F32)
    out[...] = (inv_rms * grad_gain - m[...].astype(F32) * factor).astype(BF16)


def image_grad(m, cot, gain, sums):
    rows, width = m.shape
    step = lambda i: (i, 0)
    return pl.pallas_call(
        image_grad_kernel,
        grid=(rows // LANES,),
        in_specs=[
            pl.BlockSpec((LANES, width), step),
            pl.BlockSpec((LANES, width), step),
            pl.BlockSpec((1, width), lambda i: (0, 0)),
            pl.BlockSpec((BLK, LANES), lambda i: (0, i)),
        ],
        out_specs=pl.BlockSpec((LANES, width), step),
        out_shape=struct((rows, width), BF16),
        compiler_params=params(24),
        cost_estimate=cost(6 * rows * width, 6 * rows * width),
        name="image_grad",
    )(m, cot, gain, sums)


def outputs_kernel(chunk, slot_of, m, text, cot, gain, sums, normed, grad, held, inv_col, fac_col):
    i = pl.program_id(0)

    @pl.when(i == 0)
    def _():
        held[...] = m[...].astype(F32)
        inv_rms, factor = row_factors(sums[...])
        inv_col[...] = column(inv_rms)
        fac_col[...] = column(factor)

    image = m.shape[0]
    words = text[...].astype(F32)
    grads = cot[...].astype(F32) * gain[...]
    for b in range(0, chunk, 2):
        normed_pair, grad_pair = [], []
        for c in (b, b + 1):
            local = i * chunk + c
            slot = slot_of[local]
            inside = slot >= 0
            at = pl.multiple_of(jnp.maximum(slot, 0) * BLK, BLK)
            row = pl.multiple_of(jnp.where(inside, at, image + local * BLK), BLK)
            inv_rms = inv_col[pl.ds(row, BLK), :][:, :1]
            factor = fac_col[pl.ds(row, BLK), :][:, :1]
            own = words[c * BLK : (c + 1) * BLK, :]
            merged = jnp.where(inside, held[pl.ds(at, BLK), :], own)
            slope = inv_rms * grads[c * BLK : (c + 1) * BLK, :] - merged * factor
            normed_pair.append(merged * inv_rms * gain[...])
            grad_pair.append(jnp.where(inside, 0.0, slope))
        rows = slice(b * BLK, (b + 2) * BLK)
        normed[rows, :] = jnp.concatenate(normed_pair, axis=0).astype(BF16)
        grad[rows, :] = jnp.concatenate(grad_pair, axis=0).astype(BF16)


def outputs(slot_of, m, text, cot, gain, sums):
    rows, width = text.shape
    chunk = 8
    step = lambda i: (i, 0)
    whole = lambda i: (0, 0)
    part = pl.BlockSpec((chunk * BLK, width), step)
    return pl.pallas_call(
        functools.partial(outputs_kernel, chunk),
        grid=(rows // (chunk * BLK),),
        in_specs=[
            smem(),
            pl.BlockSpec(m.shape, whole),
            part,
            part,
            pl.BlockSpec((1, width), whole),
            pl.BlockSpec(sums.shape, whole),
        ],
        out_specs=(part, part),
        out_shape=(struct((rows, width), BF16), struct((rows, width), BF16)),
        scratch_shapes=[
            pltpu.VMEM(m.shape, F32),
            pltpu.VMEM((sums.shape[1], LANES), F32),
            pltpu.VMEM((sums.shape[1], LANES), F32),
        ],
        compiler_params=params(32),
        cost_estimate=cost(10 * rows * width, 9 * rows * width),
        name="outputs",
    )(slot_of, m, text, cot, gain, sums)


def coded(values):
    most = jnp.maximum(jnp.max(jnp.abs(values), axis=0, keepdims=True), 2.0**-100)
    code = jnp.floor(jnp.log(most) * (STEPS_PER_OCTAVE / LN2)) + 2.0
    inverse = FULL / jnp.exp(code * (LN2 / STEPS_PER_OCTAVE))
    scaled = jnp.clip(jnp.floor(values * inverse + 0.5), -FULL, FULL)
    head = jnp.broadcast_to(code, (HEAD, values.shape[1]))
    return head.astype(I32).astype(I16), scaled.astype(I32).astype(I16)


def store_coded(ref, values):
    head, body = coded(values)
    ref[:HEAD, :] = head
    ref[HEAD:, :] = body


def decoded(ref):
    code = ref[:HEAD, :].astype(I32).astype(F32)[:1, :]
    scale = jnp.exp(code * (LN2 / STEPS_PER_OCTAVE)) / FULL
    return ref[HEAD:, :].astype(I32).astype(F32) * scale


def share_kernel(ranks, slots, tiles, parts, own, starts, owners, back, w, units, gains, inv, *rest):
    outs, (wide, grad_t, scaled, kept, acc) = rest[:-5], rest[-5:]
    halves = ROWS // LANES
    ups, downs, shares = outs[:halves], outs[halves : 2 * halves], outs[2 * halves :]
    i = pl.program_id(0)
    tile = w.shape[0]

    @pl.when(i == 0)
    def _():
        start = own_start_of(own[0], starts, owners, tiles)
        wide[...] = back[...].astype(F32)
        for b in range(0, TILE_BLOCKS, 16):
            group = []
            for q in range(b, b + 16):
                slot = lax.rem(start + q, ranks) * slots + q // ranks
                group.append(wide[pl.ds(pl.multiple_of(slot * BLK, BLK), BLK), :])
            rows = jnp.concatenate(group, axis=0)
            grad_t[:, b * BLK : (b + 16) * BLK] = jnp.transpose(rows).astype(BF16)
        acc[...] = jnp.zeros_like(acc)

    part = jnp.dot(w[...], grad_t[...], preferred_element_type=F32)
    at = pl.ds(pl.multiple_of(i * tile, tile), tile)
    for h in range(halves):
        lanes = slice(h * LANES, (h + 1) * LANES)
        s = part[:, lanes] * gains[...]
        u = units[:, lanes]
        scaled[at, lanes] = s
        kept[at, lanes] = u
        acc[0:1, lanes] += jnp.sum(s, axis=0, keepdims=True)
        acc[1:2, lanes] += jnp.sum(s * u, axis=0, keepdims=True)

    @pl.when(i == pl.num_programs(0) - 1)
    def _():
        size = DV // parts
        for h in range(halves):
            lanes = slice(h * LANES, (h + 1) * LANES)
            first, second = acc[0:1, lanes] / DV, acc[1:2, lanes] / DV
            scale = inv[0:1, lanes]
            for d in range(parts):
                rows = slice(d * size, (d + 1) * size)
                q = scale * (scaled[rows, lanes] - first - kept[rows, lanes] * second)
                shares[h][d, :, :] = q
                if d == 0:
                    store_coded(downs[h], q)
                if d == parts - 1:
                    store_coded(ups[h], q)


def shares_of(own, starts, owners, back, w, units, gains, inv, ranks, slots, parts):
    width = w.shape[1]
    tile = 640
    halves = ROWS // LANES
    size = DV // parts
    whole = lambda i: (0, 0)
    step = lambda i: (i, 0)
    sent = [struct((HEAD + size, LANES), I16)] * (2 * halves)
    kept = [struct((parts, size, LANES), F32)] * halves
    out = pl.pallas_call(
        functools.partial(share_kernel, ranks, slots, starts.shape[0], parts),
        grid=(DV // tile,),
        in_specs=[
            smem(),
            smem(),
            smem(),
            pl.BlockSpec(back.shape, whole),
            pl.BlockSpec((tile, width), step),
            pl.BlockSpec((tile, ROWS), step),
            pl.BlockSpec((tile, LANES), step),
            pl.BlockSpec((BLK, ROWS), whole),
        ],
        out_specs=[pl.BlockSpec((HEAD + size, LANES), whole)] * (2 * halves)
        + [pl.BlockSpec((parts, size, LANES), lambda i: (0, 0, 0))] * halves,
        out_shape=sent + kept,
        scratch_shapes=[
            pltpu.VMEM(back.shape, F32),
            pltpu.VMEM((width, ROWS), BF16),
            pltpu.VMEM((DV, ROWS), F32),
            pltpu.VMEM((DV, ROWS), F32),
            pltpu.VMEM((BLK, ROWS), F32),
        ],
        compiler_params=params(48),
        cost_estimate=cost(2 * ROWS * DV * width, 2 * DV * width + 12 * ROWS * DV),
        name="shares",
    )(own, starts, owners, back, w, units, gains, inv)
    return out[:halves], out[halves : 2 * halves], out[2 * halves :]


def relay_kernel(which, up_share, down_share, up, down, up_out, down_out):
    store_coded(up_out, up_share[0] + decoded(up))
    store_coded(down_out, down_share[0] + decoded(down))


def relay(which, share, up, down):
    parts, size, lanes = share.shape
    plain = pl.BlockSpec((HEAD + size, lanes), lambda i, which: (0, 0))
    return pl.pallas_call(
        relay_kernel,
        grid_spec=pltpu.PrefetchScalarGridSpec(
            num_scalar_prefetch=1,
            grid=(1,),
            in_specs=[
                pl.BlockSpec((1, size, lanes), lambda i, which: (which[0], 0, 0)),
                pl.BlockSpec((1, size, lanes), lambda i, which: (which[1], 0, 0)),
                plain,
                plain,
            ],
            out_specs=(plain, plain),
        ),
        out_shape=(struct((HEAD + size, lanes), I16),) * 2,
        compiler_params=params(16),
        cost_estimate=cost(20 * size * lanes, 16 * size * lanes),
        name="relay",
    )(which, share, share, up, down)


def finish_kernel(which, *refs):
    out = refs[-1]
    halves = ROWS // LANES
    for h in range(halves):
        share, up, down = refs[h], refs[halves + h], refs[2 * halves + h]
        total = share[0] + decoded(up) + decoded(down)
        out[:, h * LANES : (h + 1) * LANES] = total.astype(BF16)


def finish(which, shares, ups, downs):
    parts, size, lanes = shares[0].shape
    plain = pl.BlockSpec((HEAD + size, lanes), lambda i, which: (0, 0))
    halves = len(shares)
    return pl.pallas_call(
        finish_kernel,
        grid_spec=pltpu.PrefetchScalarGridSpec(
            num_scalar_prefetch=1,
            grid=(1,),
            in_specs=[pl.BlockSpec((1, size, lanes), lambda i, which: (which[0], 0, 0))] * halves
            + [plain] * (2 * halves),
            out_specs=pl.BlockSpec((size, halves * lanes), lambda i, which: (0, 0)),
        ),
        out_shape=struct((size, halves * lanes), BF16),
        compiler_params=params(16),
        cost_estimate=cost(20 * size * lanes, 16 * size * lanes),
        name="finish",
    )(which, *shares, *ups, *downs)


def summed(values, parts):
    if parts & (parts - 1):
        return lax.psum(values, "mp")
    hop = 1
    while hop < parts:
        values = values + lax.ppermute(values, "mp", [(i, i ^ hop) for i in range(parts)])
        hop *= 2
    return values


def exchange(rows, ranks):
    shape = rows.shape
    split = rows.reshape(ranks, shape[0] // ranks, shape[1])
    return lax.all_to_all(split, "seq", split_axis=0, concat_axis=0, tiled=True).reshape(shape)


def body(
    vit_hidden,
    vit_gain,
    vit_bias,
    proj_weight,
    text_emb,
    llm_gain,
    cotangent,
    tile_start,
    tile_owner,
):
    ranks = lax.axis_size("seq")
    parts = lax.axis_size("mp")
    own_index = lax.axis_index("seq")
    place = lax.axis_index("mp")
    slots = -(-TILE_BLOCKS // ranks)
    width = proj_weight.shape[1]
    local_blocks = text_emb.shape[0] // BLK
    own = own_index.reshape(1)
    vg, vb = vit_gain.reshape(1, DV), vit_bias.reshape(1, DV)
    gain = llm_gain.reshape(1, width)

    sent = embed(own, tile_start, tile_owner, vit_hidden, vg, vb, proj_weight, ranks, slots)
    came = exchange(sent, ranks)

    global_block = (jnp.arange(local_blocks, dtype=I32) * ranks + own_index)[:, None]
    offset = global_block - tile_start[None, :]
    covered = (offset >= 0) & (offset < TILE_BLOCKS)
    slot_of = jnp.sum(
        jnp.where(covered, tile_owner[None, :] * slots + offset // ranks + 1, 0), axis=1
    ) - 1
    owners = jnp.arange(ranks, dtype=I32)[:, None]
    start_of = jnp.sum(jnp.where(tile_owner[None, :] == owners, tile_start[None, :], 0), axis=1)
    tile_block = (own_index - start_of[:, None]) % ranks + (
        jnp.arange(slots, dtype=I32)[None, :] * ranks
    )
    local_of = jnp.minimum((start_of[:, None] + tile_block) // ranks, local_blocks - 1)
    cot_blocks = cotangent.reshape(local_blocks, BLK, width)
    cot_image = jnp.take(cot_blocks, local_of.reshape(-1), axis=0, mode="clip")
    cot_image = cot_image.reshape(-1, width)

    units, gains, inv = units_of(vit_hidden, vg)
    text_part = text_sums(text_emb, cotangent, gain)

    sums = summed(image_sums(came, cot_image, gain, text_part), parts)
    back = exchange(image_grad(came, cot_image, gain, sums), ranks)
    normed, grad_text = outputs(slot_of, came, text_emb, cotangent, gain, sums)

    ups, downs, shares = shares_of(
        own, tile_start, tile_owner, back, proj_weight, units, gains, inv, ranks, slots, parts
    )
    last = parts - 1
    for s in range(1, parts):
        up_pairs = [(z, z + 1) for z in range(s)]
        down_pairs = [(last - z, last - z - 1) for z in range(s)]
        ups = [lax.ppermute(u, "mp", up_pairs) for u in ups]
        downs = [lax.ppermute(d, "mp", down_pairs) for d in downs]
        if s < last:
            which = jnp.stack(
                [jnp.minimum(last - s + place, last), jnp.maximum(place - last + s, 0)]
            )
            both = [relay(which, q, u, d) for q, u, d in zip(shares, ups, downs)]
            ups, downs = [b[0] for b in both], [b[1] for b in both]
    grad_vit = finish(place.reshape(1), shares, ups, downs)
    return (normed, grad_text, grad_vit.T)


def solution(mesh):
    in_specs = (
        P("seq", None),
        P(),
        P(),
        P(None, "mp"),
        P("seq", "mp"),
        P("mp"),
        P("seq", "mp"),
        P(),
        P(),
    )
    out_specs = (P("seq", "mp"), P("seq", "mp"), P("seq", "mp"))
    return jax.shard_map(body, mesh=mesh, in_specs=in_specs, out_specs=out_specs, check_vma=False)
```

```python
import functools

import jax
import jax.numpy as jnp
from jax import lax
from jax.experimental import pallas as pl
from jax.experimental.pallas import tpu as pltpu
from jax.sharding import PartitionSpec as P

D = 8192
DV = 3200
BLK = 8
TILE_BLOCKS = 32
ROWS = TILE_BLOCKS * BLK
EPSILON = 1e-05
LANES = 128
HEAD = 16
FULL = 32767.0
STEPS_PER_OCTAVE = 16.0
LN2 = 0.6931471805599453
F32 = jnp.float32
BF16 = jnp.bfloat16
I32 = jnp.int32
I16 = jnp.int16


def struct(shape, kind):
    return jax.ShapeDtypeStruct(shape, kind)


def smem():
    return pl.BlockSpec(memory_space=pltpu.SMEM)


def params():
    return pltpu.CompilerParams(vmem_limit_bytes=67043328)


def cost(flops, moved):
    return pl.CostEstimate(flops=int(flops), bytes_accessed=int(moved), transcendentals=0)


def column(row):
    return jnp.transpose(jnp.broadcast_to(row, (LANES, row.shape[1])))


def as_row(col):
    return jnp.transpose(jnp.broadcast_to(col, (col.shape[0], LANES)))


def own_start_of(own, starts, owners, tiles):
    found = starts[0]
    for t in range(1, tiles):
        found = jnp.where(owners[t] == own, starts[t], found)
    return found


def norm_stats(values):
    mean = jnp.mean(values, axis=1, keepdims=True)
    centred = values - mean
    inv_std = lax.rsqrt(jnp.mean(centred * centred, axis=1, keepdims=True) + EPSILON)
    return mean, centred, inv_std


def embed_kernel(ranks, slots, tiles, own, starts, owners, x, vg, vb, w, out, natural, ordered):
    @pl.when(pl.program_id(0) == 0)
    def _():
        start = own_start_of(own[0], starts, owners, tiles)
        for c in range(0, ROWS, 64):
            _, centred, inv_std = norm_stats(x[c : c + 64, :].astype(F32))
            normed = (centred * inv_std * vg[...] + vb[...]).astype(BF16)
            natural[c : c + 64, :] = normed.astype(F32)
        for p in range(0, ranks * slots, 2):
            pair = []
            for q in (p, p + 1):
                block = lax.rem(q // slots - start + ranks * 1024, ranks) + (q % slots) * ranks
                block = jnp.minimum(block, TILE_BLOCKS - 1)
                pair.append(natural[pl.ds(pl.multiple_of(block * BLK, BLK), BLK), :])
            ordered[p * BLK : (p + 2) * BLK, :] = jnp.concatenate(pair, axis=0).astype(BF16)

    out[...] = jnp.dot(ordered[...], w[...], preferred_element_type=F32).astype(BF16)


def embed(own, starts, owners, x, vg, vb, w, ranks, slots):
    width = w.shape[1]
    tile = min(256, width)
    rows = ranks * slots * BLK
    whole = lambda i: (0, 0)
    return pl.pallas_call(
        functools.partial(embed_kernel, ranks, slots, starts.shape[0]),
        grid=(width // tile,),
        in_specs=[
            smem(),
            smem(),
            smem(),
            pl.BlockSpec((ROWS, DV), whole),
            pl.BlockSpec((1, DV), whole),
            pl.BlockSpec((1, DV), whole),
            pl.BlockSpec((DV, tile), lambda i: (0, i)),
        ],
        out_specs=pl.BlockSpec((rows, tile), lambda i: (0, i)),
        out_shape=struct((rows, width), BF16),
        scratch_shapes=[pltpu.VMEM((ROWS, DV), F32), pltpu.VMEM((rows, DV), BF16)],
        compiler_params=params(),
        cost_estimate=cost(2 * rows * DV * width, 2 * DV * width + 4 * ROWS * DV),
        name="embed",
    )(own, starts, owners, x, vg, vb, w)


def units_kernel(x, vg, units, gains, inv):
    mean, _, inv_std = norm_stats(x[...].astype(F32))
    inv[...] = as_row(inv_std)[:BLK, :]
    for c in range(0, DV, 640):
        part = (x[:, c : c + 640].astype(F32) - mean) * inv_std
        units[c : c + 640, :] = jnp.transpose(part)
        gains[c : c + 640, :] = column(vg[:, c : c + 640])


def units_of(x, vg):
    return pl.pallas_call(
        units_kernel,
        out_shape=(struct((DV, ROWS), F32), struct((DV, LANES), F32), struct((BLK, ROWS), F32)),
        compiler_params=params(),
        cost_estimate=cost(10 * ROWS * DV, 8 * ROWS * DV),
        name="units",
    )(x, vg)


def sums_of(m, gc):
    squares = as_row(jnp.sum(m * m, axis=1, keepdims=True))[:BLK, :]
    products = as_row(jnp.sum(gc * m, axis=1, keepdims=True))[:BLK, :]
    first = lax.broadcasted_iota(I32, squares.shape, 0) == 0
    return jnp.where(first, squares, products)


def text_sums_kernel(text, cot, gain, out):
    out[...] = sums_of(text[...].astype(F32), gain[...] * cot[...].astype(F32))


def text_sums(text, cot, gain):
    rows, width = text.shape
    step = lambda i: (i, 0)
    return pl.pallas_call(
        text_sums_kernel,
        grid=(rows // LANES,),
        in_specs=[
            pl.BlockSpec((LANES, width), step),
            pl.BlockSpec((LANES, width), step),
            pl.BlockSpec((1, width), lambda i: (0, 0)),
        ],
        out_specs=pl.BlockSpec((BLK, LANES), lambda i: (0, i)),
        out_shape=struct((BLK, rows), F32),
        compiler_params=params(),
        cost_estimate=cost(6 * rows * width, 4 * rows * width),
        name="text_sums",
    )(text, cot, gain)


def image_sums_kernel(image, m, cot, gain, text, after, out):
    i = pl.program_id(0)

    @pl.when(i == 0)
    def _():
        out[:, image:] = text[...]

    found = sums_of(m[...].astype(F32), gain[...] * cot[...].astype(F32))
    out[:, pl.ds(pl.multiple_of(i * LANES, LANES), LANES)] = found


def image_sums(m, cot, gain, text, after):
    rows, width = m.shape
    total = rows + text.shape[1]
    step = lambda i: (i, 0)
    whole = lambda i: (0, 0)
    return pl.pallas_call(
        functools.partial(image_sums_kernel, rows),
        grid=(rows // LANES,),
        in_specs=[
            pl.BlockSpec((LANES, width), step),
            pl.BlockSpec((LANES, width), step),
            pl.BlockSpec((1, width), whole),
            pl.BlockSpec((BLK, text.shape[1]), whole),
            pl.BlockSpec((BLK, LANES), whole),
        ],
        out_specs=pl.BlockSpec((BLK, total), whole),
        out_shape=struct((BLK, total), F32),
        compiler_params=params(),
        cost_estimate=cost(6 * rows * width, 4 * rows * width),
        name="image_sums",
    )(m, cot, gain, text, after)


def row_factors(sums):
    inv_rms = lax.rsqrt(sums[0:1, :] / D + EPSILON)
    return inv_rms, inv_rms * inv_rms * inv_rms * sums[1:2, :] / D


def image_grad_kernel(m, cot, gain, sums, out):
    inv_rms, factor = row_factors(sums[...])
    inv_rms, factor = column(inv_rms)[:, :1], column(factor)[:, :1]
    grad_gain = gain[...] * cot[...].astype(F32)
    out[...] = (inv_rms * grad_gain - m[...].astype(F32) * factor).astype(BF16)


def image_grad(m, cot, gain, sums):
    rows, width = m.shape
    step = lambda i: (i, 0)
    return pl.pallas_call(
        image_grad_kernel,
        grid=(rows // LANES,),
        in_specs=[
            pl.BlockSpec((LANES, width), step),
            pl.BlockSpec((LANES, width), step),
            pl.BlockSpec((1, width), lambda i: (0, 0)),
            pl.BlockSpec((BLK, LANES), lambda i: (0, i)),
        ],
        out_specs=pl.BlockSpec((LANES, width), step),
        out_shape=struct((rows, width), BF16),
        compiler_params=params(),
        cost_estimate=cost(6 * rows * width, 6 * rows * width),
        name="image_grad",
    )(m, cot, gain, sums)


def outputs_kernel(
    chunk, slot_of, m, text, cot, gain, sums, normed, grad, token, held, inv_col, fac_col
):
    i = pl.program_id(0)

    @pl.when(i == 0)
    def _():
        held[...] = m[...].astype(F32)
        token[...] = jnp.zeros_like(token)
        inv_rms, factor = row_factors(sums[...])
        inv_col[...] = column(inv_rms)
        fac_col[...] = column(factor)

    image = m.shape[0]
    words = text[...].astype(F32)
    grads = cot[...].astype(F32) * gain[...]
    for b in range(0, chunk, 2):
        normed_pair, grad_pair = [], []
        for c in (b, b + 1):
            local = i * chunk + c
            slot = slot_of[local]
            inside = slot >= 0
            at = pl.multiple_of(jnp.maximum(slot, 0) * BLK, BLK)
            row = pl.multiple_of(jnp.where(inside, at, image + local * BLK), BLK)
            inv_rms = inv_col[pl.ds(row, BLK), :][:, :1]
            factor = fac_col[pl.ds(row, BLK), :][:, :1]
            own = words[c * BLK : (c + 1) * BLK, :]
            merged = jnp.where(inside, held[pl.ds(at, BLK), :], own)
            slope = inv_rms * grads[c * BLK : (c + 1) * BLK, :] - merged * factor
            normed_pair.append(merged * inv_rms * gain[...])
            grad_pair.append(jnp.where(inside, 0.0, slope))
        rows = slice(b * BLK, (b + 2) * BLK)
        normed[rows, :] = jnp.concatenate(normed_pair, axis=0).astype(BF16)
        grad[rows, :] = jnp.concatenate(grad_pair, axis=0).astype(BF16)


def outputs(slot_of, m, text, cot, gain, sums):
    rows, width = text.shape
    chunk = 8
    step = lambda i: (i, 0)
    whole = lambda i: (0, 0)
    part = pl.BlockSpec((chunk * BLK, width), step)
    return pl.pallas_call(
        functools.partial(outputs_kernel, chunk),
        grid=(rows // (chunk * BLK),),
        in_specs=[
            smem(),
            pl.BlockSpec(m.shape, whole),
            part,
            part,
            pl.BlockSpec((1, width), whole),
            pl.BlockSpec(sums.shape, whole),
        ],
        out_specs=(part, part, pl.BlockSpec((BLK, LANES), whole)),
        out_shape=(
            struct((rows, width), BF16),
            struct((rows, width), BF16),
            struct((BLK, LANES), F32),
        ),
        scratch_shapes=[
            pltpu.VMEM(m.shape, F32),
            pltpu.VMEM((sums.shape[1], LANES), F32),
            pltpu.VMEM((sums.shape[1], LANES), F32),
        ],
        compiler_params=params(),
        cost_estimate=cost(10 * rows * width, 9 * rows * width),
        name="outputs",
    )(slot_of, m, text, cot, gain, sums)


def coded(values):
    most = jnp.maximum(jnp.max(jnp.abs(values), axis=0, keepdims=True), 2.0**-100)
    code = jnp.floor(jnp.log(most) * (STEPS_PER_OCTAVE / LN2)) + 2.0
    inverse = FULL / jnp.exp(code * (LN2 / STEPS_PER_OCTAVE))
    scaled = jnp.clip(jnp.floor(values * inverse + 0.5), -FULL, FULL)
    head = jnp.broadcast_to(code, (HEAD, values.shape[1]))
    return head.astype(I32).astype(I16), scaled.astype(I32).astype(I16)


def store_coded(ref, values):
    head, body = coded(values)
    ref[:HEAD, :] = head
    ref[HEAD:, :] = body


def decoded(ref):
    code = ref[:HEAD, :].astype(I32).astype(F32)[:1, :]
    scale = jnp.exp(code * (LN2 / STEPS_PER_OCTAVE)) / FULL
    return ref[HEAD:, :].astype(I32).astype(F32) * scale


def share_kernel(
    ranks, slots, tiles, parts, own, starts, owners, which, back, w, units, gains, inv, after,
    first, second, shares, wide, grad_t, scaled, kept, acc
):
    i = pl.program_id(0)
    tile = w.shape[0]

    @pl.when(i == 0)
    def _():
        start = own_start_of(own[0], starts, owners, tiles)
        wide[...] = back[...].astype(F32)
        for b in range(0, TILE_BLOCKS, 16):
            group = []
            for q in range(b, b + 16):
                slot = lax.rem(start + q, ranks) * slots + q // ranks
                group.append(wide[pl.ds(pl.multiple_of(slot * BLK, BLK), BLK), :])
            rows = jnp.concatenate(group, axis=0)
            grad_t[:, b * BLK : (b + 16) * BLK] = jnp.transpose(rows).astype(BF16)
        acc[...] = jnp.zeros_like(acc)

    part = jnp.dot(w[...], grad_t[...], preferred_element_type=F32)
    at = pl.ds(pl.multiple_of(i * tile, tile), tile)
    for lanes in (slice(0, LANES), slice(LANES, 2 * LANES)):
        s = part[:, lanes] * gains[...]
        u = units[:, lanes]
        scaled[at, lanes] = s
        kept[at, lanes] = u
        acc[0:1, lanes] += jnp.sum(s, axis=0, keepdims=True)
        acc[1:2, lanes] += jnp.sum(s * u, axis=0, keepdims=True)

    @pl.when(i == pl.num_programs(0) - 1)
    def _():
        size = DV // parts
        mean, slope, scale = acc[0:1, :] / DV, acc[1:2, :] / DV, inv[0:1, :]
        for d in range(parts):
            rows = slice(d * size, (d + 1) * size)
            shares[d, :, :] = scale * (scaled[rows, :] - mean - kept[rows, :] * slope)
        store_coded(first, shares[which[0]])
        store_coded(second, shares[which[1]])


def shares_of(
    own, starts, owners, which, back, w, units, gains, inv, after, ranks, slots, parts
):
    width = w.shape[1]
    tile = 640
    size = DV // parts
    whole = lambda i: (0, 0)
    step = lambda i: (i, 0)
    sent = struct((HEAD + size, ROWS), I16)
    return pl.pallas_call(
        functools.partial(share_kernel, ranks, slots, starts.shape[0], parts),
        grid=(DV // tile,),
        in_specs=[
            smem(),
            smem(),
            smem(),
            smem(),
            pl.BlockSpec(back.shape, whole),
            pl.BlockSpec((tile, width), step),
            pl.BlockSpec((tile, ROWS), step),
            pl.BlockSpec((tile, LANES), step),
            pl.BlockSpec((BLK, ROWS), whole),
            pl.BlockSpec((BLK, LANES), whole),
        ],
        out_specs=(
            pl.BlockSpec((HEAD + size, ROWS), whole),
            pl.BlockSpec((HEAD + size, ROWS), whole),
            pl.BlockSpec((parts, size, ROWS), lambda i: (0, 0, 0)),
        ),
        out_shape=(sent, sent, struct((parts, size, ROWS), F32)),
        scratch_shapes=[
            pltpu.VMEM(back.shape, F32),
            pltpu.VMEM((width, ROWS), BF16),
            pltpu.VMEM((DV, ROWS), F32),
            pltpu.VMEM((DV, ROWS), F32),
            pltpu.VMEM((BLK, ROWS), F32),
        ],
        compiler_params=params(),
        cost_estimate=cost(2 * ROWS * DV * width, 2 * DV * width + 12 * ROWS * DV),
        name="shares",
    )(own, starts, owners, which, back, w, units, gains, inv, after)


def relay_kernel(which, share, came, out):
    store_coded(out, share[0] + decoded(came))


def relay(which, share, came):
    parts, size, lanes = share.shape
    plain = pl.BlockSpec((HEAD + size, lanes), lambda i, which: (0, 0))
    return pl.pallas_call(
        relay_kernel,
        grid_spec=pltpu.PrefetchScalarGridSpec(
            num_scalar_prefetch=1,
            grid=(1,),
            in_specs=[
                pl.BlockSpec((1, size, lanes), lambda i, which: (which[0], 0, 0)),
                plain,
            ],
            out_specs=plain,
        ),
        out_shape=struct((HEAD + size, lanes), I16),
        compiler_params=params(),
        cost_estimate=cost(20 * size * lanes, 8 * size * lanes),
        name="relay",
    )(which.reshape(1), share, came)


def finish_kernel(which, share, one, other, out):
    out[...] = (share[0] + decoded(one) + decoded(other)).astype(BF16)


def finish(which, share, one, other):
    parts, size, lanes = share.shape
    plain = pl.BlockSpec((HEAD + size, lanes), lambda i, which: (0, 0))
    return pl.pallas_call(
        finish_kernel,
        grid_spec=pltpu.PrefetchScalarGridSpec(
            num_scalar_prefetch=1,
            grid=(1,),
            in_specs=[
                pl.BlockSpec((1, size, lanes), lambda i, which: (which[0], 0, 0)),
                plain,
                plain,
            ],
            out_specs=pl.BlockSpec((size, lanes), lambda i, which: (0, 0)),
        ),
        out_shape=struct((size, lanes), BF16),
        compiler_params=params(),
        cost_estimate=cost(20 * size * lanes, 8 * size * lanes),
        name="finish",
    )(which.reshape(1), share, one, other)


def first_chunks(place, parts):
    last = parts - 1
    if parts == 4:
        low = place < 2
        return jnp.stack([jnp.where(low, last, 0), jnp.where(low, last - 1, 1)])
    return jnp.stack([jnp.full_like(place, last), jnp.zeros_like(place)])


def scatter_sum(first, second, share, place, parts):
    last = parts - 1
    if parts == 4:
        low = place < 2
        outer, inner = [(0, 1), (3, 2)], [(1, 2), (2, 1)]
        a = lax.ppermute(first, "mp", outer)
        b = lax.ppermute(second, "mp", outer)
        c = lax.ppermute(relay(jnp.where(low, 3, 0), share, a), "mp", inner)
        d = lax.ppermute(relay(jnp.where(low, 2, 1), share, b), "mp", inner)
        turn = place + 1 - 2 * (place % 2)
        pairs = [(0, 1), (1, 0), (2, 3), (3, 2)]
        e = lax.ppermute(relay(turn, share, c), "mp", pairs)
        return finish(place, share, d, e)
    up, down = first, second
    for s in range(1, parts):
        up = lax.ppermute(up, "mp", [(z, z + 1) for z in range(s)])
        down = lax.ppermute(down, "mp", [(last - z, last - z - 1) for z in range(s)])
        if s < last:
            up = relay(jnp.minimum(last - s + place, last), share, up)
            down = relay(jnp.maximum(place - last + s, 0), share, down)
    return finish(place, share, up, down)


def summed(values, parts):
    if parts & (parts - 1):
        return lax.psum(values, "mp")
    hop = 1
    while hop < parts:
        values = values + lax.ppermute(values, "mp", [(i, i ^ hop) for i in range(parts)])
        hop *= 2
    return values


def exchange(rows, ranks):
    shape = rows.shape
    split = rows.reshape(ranks, shape[0] // ranks, shape[1])
    return lax.all_to_all(split, "seq", split_axis=0, concat_axis=0, tiled=True).reshape(shape)


def body(
    vit_hidden,
    vit_gain,
    vit_bias,
    proj_weight,
    text_emb,
    llm_gain,
    cotangent,
    tile_start,
    tile_owner,
):
    ranks = lax.axis_size("seq")
    parts = lax.axis_size("mp")
    own_index = lax.axis_index("seq")
    place = lax.axis_index("mp")
    slots = -(-TILE_BLOCKS // ranks)
    width = proj_weight.shape[1]
    local_blocks = text_emb.shape[0] // BLK
    own = own_index.reshape(1)
    vg, vb = vit_gain.reshape(1, DV), vit_bias.reshape(1, DV)
    gain = llm_gain.reshape(1, width)

    sent = embed(own, tile_start, tile_owner, vit_hidden, vg, vb, proj_weight, ranks, slots)
    came = exchange(sent, ranks)

    global_block = (jnp.arange(local_blocks, dtype=I32) * ranks + own_index)[:, None]
    offset = global_block - tile_start[None, :]
    covered = (offset >= 0) & (offset < TILE_BLOCKS)
    slot_of = jnp.sum(
        jnp.where(covered, tile_owner[None, :] * slots + offset // ranks + 1, 0), axis=1
    ) - 1
    owners = jnp.arange(ranks, dtype=I32)[:, None]
    start_of = jnp.sum(jnp.where(tile_owner[None, :] == owners, tile_start[None, :], 0), axis=1)
    tile_block = (own_index - start_of[:, None]) % ranks + (
        jnp.arange(slots, dtype=I32)[None, :] * ranks
    )
    local_of = jnp.minimum((start_of[:, None] + tile_block) // ranks, local_blocks - 1)
    cot_blocks = cotangent.reshape(local_blocks, BLK, width)
    cot_image = jnp.take(cot_blocks, local_of.reshape(-1), axis=0, mode="clip")
    cot_image = cot_image.reshape(-1, width)

    units, gains, inv = units_of(vit_hidden, vg)
    text_part = text_sums(text_emb, cotangent, gain)

    sums = summed(image_sums(came, cot_image, gain, text_part, inv), parts)
    back = exchange(image_grad(came, cot_image, gain, sums), ranks)
    normed, grad_text, after = outputs(slot_of, came, text_emb, cotangent, gain, sums)

    which = first_chunks(place, parts)
    first, second, share = shares_of(
        own, tile_start, tile_owner, which, back, proj_weight, units, gains, inv, after,
        ranks, slots, parts
    )
    grad_vit = scatter_sum(first, second, share, place, parts)
    return (normed, grad_text, grad_vit.T)


def solution(mesh):
    in_specs = (
        P("seq", None),
        P(),
        P(),
        P(None, "mp"),
        P("seq", "mp"),
        P("mp"),
        P("seq", "mp"),
        P(),
        P(),
    )
    out_specs = (P("seq", "mp"), P("seq", "mp"), P("seq", "mp"))
    return jax.shard_map(body, mesh=mesh, in_specs=in_specs, out_specs=out_specs, check_vma=False)
```

```python
import functools

import jax
import jax.numpy as jnp
from jax import lax
from jax.experimental import pallas as pl
from jax.experimental.pallas import tpu as pltpu
from jax.sharding import PartitionSpec as P

D = 8192
DV = 3200
BLK = 8
TILE_BLOCKS = 32
ROWS = TILE_BLOCKS * BLK
EPSILON = 1e-05
LANES = 128
HEAD = 16
FULL = 32767.0
STEPS_PER_OCTAVE = 16.0
LN2 = 0.6931471805599453
F32 = jnp.float32
BF16 = jnp.bfloat16
I32 = jnp.int32
I16 = jnp.int16


def struct(shape, kind):
    return jax.ShapeDtypeStruct(shape, kind)


def smem():
    return pl.BlockSpec(memory_space=pltpu.SMEM)


def params(mib=16):
    return pltpu.CompilerParams(vmem_limit_bytes=mib << 20)


def cost(flops, moved):
    return pl.CostEstimate(flops=int(flops), bytes_accessed=int(moved), transcendentals=0)


def column(row):
    return jnp.transpose(jnp.broadcast_to(row, (LANES, row.shape[1])))


def as_row(col):
    return jnp.transpose(jnp.broadcast_to(col, (col.shape[0], LANES)))


def own_start_of(own, starts, owners, tiles):
    found = starts[0]
    for t in range(1, tiles):
        found = jnp.where(owners[t] == own, starts[t], found)
    return found


def norm_stats(values):
    mean = jnp.mean(values, axis=1, keepdims=True)
    centred = values - mean
    inv_std = lax.rsqrt(jnp.mean(centred * centred, axis=1, keepdims=True) + EPSILON)
    return mean, centred, inv_std


def embed_kernel(
    ranks, slots, tiles, own, starts, owners, x, vg, vb, w, out, natural, ordered, held, made, sems
):
    pieces = held.shape[0]
    tile = held.shape[2]
    coming = [
        pltpu.make_async_copy(w.at[:, i * tile : (i + 1) * tile], held.at[i], sems.at[i])
        for i in range(pieces)
    ]
    for copy in coming:
        copy.start()
    start = own_start_of(own[0], starts, owners, tiles)
    gain, bias = vg[...].reshape(1, DV), vb[...].reshape(1, DV)
    for c in range(0, ROWS, 64):
        _, centred, inv_std = norm_stats(x[c : c + 64, :].astype(F32))
        normed = (centred * inv_std * gain + bias).astype(BF16)
        natural[c : c + 64, :] = normed.astype(F32)
    for p in range(0, ranks * slots, 2):
        pair = []
        for q in (p, p + 1):
            block = lax.rem(q // slots - start + ranks * 1024, ranks) + (q % slots) * ranks
            block = jnp.minimum(block, TILE_BLOCKS - 1)
            pair.append(natural[pl.ds(pl.multiple_of(block * BLK, BLK), BLK), :])
        ordered[p * BLK : (p + 2) * BLK, :] = jnp.concatenate(pair, axis=0).astype(BF16)
    going = []
    for i in range(pieces):
        coming[i].wait()
        made[i, :, :] = jnp.dot(ordered[...], held[i], preferred_element_type=F32).astype(BF16)
        going.append(
            pltpu.make_async_copy(
                made.at[i], out.at[:, i * tile : (i + 1) * tile], sems.at[pieces + i]
            )
        )
        going[i].start()
    for copy in going:
        copy.wait()


def embed(own, starts, owners, x, vg, vb, w, ranks, slots):
    width = w.shape[1]
    pieces = 4
    tile = width // pieces
    rows = ranks * slots * BLK
    vmem = pl.BlockSpec(memory_space=pltpu.VMEM)
    anywhere = pl.BlockSpec(memory_space=pl.ANY)
    return pl.pallas_call(
        functools.partial(embed_kernel, ranks, slots, starts.shape[0]),
        in_specs=[smem(), smem(), smem(), vmem, vmem, vmem, anywhere],
        out_specs=anywhere,
        out_shape=struct((rows, width), BF16),
        scratch_shapes=[
            pltpu.VMEM((ROWS, DV), F32),
            pltpu.VMEM((rows, DV), BF16),
            pltpu.VMEM((pieces, DV, tile), BF16),
            pltpu.VMEM((pieces, rows, tile), BF16),
            pltpu.SemaphoreType.DMA((2 * pieces,)),
        ],
        compiler_params=params(63),
        cost_estimate=cost(2 * rows * DV * width, 2 * DV * width + 4 * ROWS * DV),
        name="embed",
    )(own, starts, owners, x, vg, vb, w)


def units_kernel(x, vg, after, units, gains, inv):
    mean, _, inv_std = norm_stats(x[...].astype(F32))
    inv[...] = as_row(inv_std)[:BLK, :]
    gain = vg[...].reshape(1, DV)
    for c in range(0, DV, 640):
        part = (x[:, c : c + 640].astype(F32) - mean) * inv_std
        units[c : c + 640, :] = jnp.transpose(part)
        gains[c : c + 640, :] = column(gain[:, c : c + 640])


def units_of(x, vg, after):
    return pl.pallas_call(
        units_kernel,
        out_shape=(struct((DV, ROWS), F32), struct((DV, LANES), F32), struct((BLK, ROWS), F32)),
        compiler_params=params(32),
        cost_estimate=cost(10 * ROWS * DV, 8 * ROWS * DV),
        name="units",
    )(x, vg, after)


def sums_of(m, gc):
    squares = as_row(jnp.sum(m * m, axis=1, keepdims=True))[:BLK, :]
    products = as_row(jnp.sum(gc * m, axis=1, keepdims=True))[:BLK, :]
    first = lax.broadcasted_iota(I32, squares.shape, 0) == 0
    return jnp.where(first, squares, products)


def text_sums_kernel(text, cot, gain, out):
    out[...] = sums_of(text[...].astype(F32), gain[...] * cot[...].astype(F32))


def text_sums(text, cot, gain):
    rows, width = text.shape
    step = lambda i: (i, 0)
    return pl.pallas_call(
        text_sums_kernel,
        grid=(rows // LANES,),
        in_specs=[
            pl.BlockSpec((LANES, width), step),
            pl.BlockSpec((LANES, width), step),
            pl.BlockSpec((1, width), lambda i: (0, 0)),
        ],
        out_specs=pl.BlockSpec((BLK, LANES), lambda i: (0, i)),
        out_shape=struct((BLK, rows), F32),
        compiler_params=params(),
        cost_estimate=cost(6 * rows * width, 4 * rows * width),
        name="text_sums",
    )(text, cot, gain)


def image_sums_kernel(image, m, cot, gain, text, out):
    i = pl.program_id(0)

    @pl.when(i == 0)
    def _():
        out[:, image:] = text[...]

    found = sums_of(m[...].astype(F32), gain[...] * cot[...].astype(F32))
    out[:, pl.ds(pl.multiple_of(i * LANES, LANES), LANES)] = found


def image_sums(m, cot, gain, text):
    rows, width = m.shape
    total = rows + text.shape[1]
    step = lambda i: (i, 0)
    whole = lambda i: (0, 0)
    return pl.pallas_call(
        functools.partial(image_sums_kernel, rows),
        grid=(rows // LANES,),
        in_specs=[
            pl.BlockSpec((LANES, width), step),
            pl.BlockSpec((LANES, width), step),
            pl.BlockSpec((1, width), whole),
            pl.BlockSpec((BLK, text.shape[1]), whole),
        ],
        out_specs=pl.BlockSpec((BLK, total), whole),
        out_shape=struct((BLK, total), F32),
        compiler_params=params(),
        cost_estimate=cost(6 * rows * width, 4 * rows * width),
        name="image_sums",
    )(m, cot, gain, text)


def row_factors(sums):
    inv_rms = lax.rsqrt(sums[0:1, :] / D + EPSILON)
    return inv_rms, inv_rms * inv_rms * inv_rms * sums[1:2, :] / D


def image_grad_kernel(m, cot, gain, sums, out):
    inv_rms, factor = row_factors(sums[...])
    inv_rms, factor = column(inv_rms)[:, :1], column(factor)[:, :1]
    grad_gain = gain[...] * cot[...].astype(F32)
    out[...] = (inv_rms * grad_gain - m[...].astype(F32) * factor).astype(BF16)


def image_grad(m, cot, gain, sums):
    rows, width = m.shape
    step = lambda i: (i, 0)
    return pl.pallas_call(
        image_grad_kernel,
        grid=(rows // LANES,),
        in_specs=[
            pl.BlockSpec((LANES, width), step),
            pl.BlockSpec((LANES, width), step),
            pl.BlockSpec((1, width), lambda i: (0, 0)),
            pl.BlockSpec((BLK, LANES), lambda i: (0, i)),
        ],
        out_specs=pl.BlockSpec((LANES, width), step),
        out_shape=struct((rows, width), BF16),
        compiler_params=params(),
        cost_estimate=cost(6 * rows * width, 6 * rows * width),
        name="image_grad",
    )(m, cot, gain, sums)


def outputs_kernel(
    chunk, slot_of, m, text, cot, gain, sums, normed, grad, token, held, inv_col, fac_col
):
    i = pl.program_id(0)

    @pl.when(i == 0)
    def _():
        held[...] = m[...].astype(F32)
        token[...] = jnp.zeros_like(token)
        inv_rms, factor = row_factors(sums[...])
        inv_col[...] = column(inv_rms)
        fac_col[...] = column(factor)

    image = m.shape[0]
    words = text[...].astype(F32)
    grads = cot[...].astype(F32) * gain[...]
    for b in range(0, chunk, 2):
        normed_pair, grad_pair = [], []
        for c in (b, b + 1):
            local = i * chunk + c
            slot = slot_of[local]
            inside = slot >= 0
            at = pl.multiple_of(jnp.maximum(slot, 0) * BLK, BLK)
            row = pl.multiple_of(jnp.where(inside, at, image + local * BLK), BLK)
            inv_rms = inv_col[pl.ds(row, BLK), :][:, :1]
            factor = fac_col[pl.ds(row, BLK), :][:, :1]
            own = words[c * BLK : (c + 1) * BLK, :]
            merged = jnp.where(inside, held[pl.ds(at, BLK), :], own)
            slope = inv_rms * grads[c * BLK : (c + 1) * BLK, :] - merged * factor
            normed_pair.append(merged * inv_rms * gain[...])
            grad_pair.append(jnp.where(inside, 0.0, slope))
        rows = slice(b * BLK, (b + 2) * BLK)
        normed[rows, :] = jnp.concatenate(normed_pair, axis=0).astype(BF16)
        grad[rows, :] = jnp.concatenate(grad_pair, axis=0).astype(BF16)


def outputs(slot_of, m, text, cot, gain, sums):
    rows, width = text.shape
    chunk = 8
    step = lambda i: (i, 0)
    whole = lambda i: (0, 0)
    part = pl.BlockSpec((chunk * BLK, width), step)
    return pl.pallas_call(
        functools.partial(outputs_kernel, chunk),
        grid=(rows // (chunk * BLK),),
        in_specs=[
            smem(),
            pl.BlockSpec(m.shape, whole),
            part,
            part,
            pl.BlockSpec((1, width), whole),
            pl.BlockSpec(sums.shape, whole),
        ],
        out_specs=(part, part, pl.BlockSpec((BLK, LANES), whole)),
        out_shape=(
            struct((rows, width), BF16),
            struct((rows, width), BF16),
            struct((BLK, LANES), F32),
        ),
        scratch_shapes=[
            pltpu.VMEM(m.shape, F32),
            pltpu.VMEM((sums.shape[1], LANES), F32),
            pltpu.VMEM((sums.shape[1], LANES), F32),
        ],
        compiler_params=params(24),
        cost_estimate=cost(10 * rows * width, 9 * rows * width),
        name="outputs",
    )(slot_of, m, text, cot, gain, sums)


def coded(values):
    most = jnp.maximum(jnp.max(jnp.abs(values), axis=0, keepdims=True), 2.0**-100)
    code = jnp.floor(jnp.log(most) * (STEPS_PER_OCTAVE / LN2)) + 2.0
    inverse = FULL / jnp.exp(code * (LN2 / STEPS_PER_OCTAVE))
    scaled = jnp.clip(jnp.floor(values * inverse + 0.5), -FULL, FULL)
    head = jnp.broadcast_to(code, (HEAD, values.shape[1]))
    return head.astype(I32).astype(I16), scaled.astype(I32).astype(I16)


def store_coded(ref, values):
    head, body = coded(values)
    ref[:HEAD, :] = head
    ref[HEAD:, :] = body


def decoded(ref):
    code = ref[:HEAD, :].astype(I32).astype(F32)[:1, :]
    scale = jnp.exp(code * (LN2 / STEPS_PER_OCTAVE)) / FULL
    return ref[HEAD:, :].astype(I32).astype(F32) * scale


def share_of(scaled, units, stats):
    mean, slope, scale = stats[0:1, :], stats[1:2, :], stats[2:3, :]
    return scale * (scaled - mean - units * slope)


def scaled_kernel(
    ranks, slots, tiles, own, starts, owners, which, back, w, units, gains, inv,
    scaled, stats, first, wide, grad_t, held, sems
):
    pieces, tile = held.shape[0], held.shape[1]
    coming = [
        pltpu.make_async_copy(w.at[i * tile : (i + 1) * tile, :], held.at[i], sems.at[i])
        for i in range(pieces)
    ]
    for copy in coming:
        copy.start()
    start = own_start_of(own[0], starts, owners, tiles)
    wide[...] = back[...].astype(F32)
    for b in range(0, TILE_BLOCKS, 16):
        group = []
        for q in range(b, b + 16):
            slot = lax.rem(start + q, ranks) * slots + q // ranks
            group.append(wide[pl.ds(pl.multiple_of(slot * BLK, BLK), BLK), :])
        rows = jnp.concatenate(group, axis=0)
        grad_t[:, b * BLK : (b + 16) * BLK] = jnp.transpose(rows).astype(BF16)
    total = jnp.zeros((1, ROWS), F32)
    along = jnp.zeros((1, ROWS), F32)
    for i in range(pieces):
        coming[i].wait()
        at = slice(i * tile, (i + 1) * tile)
        part = jnp.dot(held[i], grad_t[...], preferred_element_type=F32)
        s = part * jnp.concatenate([gains[at, :], gains[at, :]], axis=1)
        scaled[at, :] = s
        total = total + jnp.sum(s, axis=0, keepdims=True)
        along = along + jnp.sum(s * units[at, :], axis=0, keepdims=True)
    rest = jnp.zeros((BLK - 3, ROWS), F32)
    stats[...] = jnp.concatenate([total / DV, along / DV, inv[0:1, :], rest], axis=0)
    size = first.shape[0] - HEAD
    at = pl.ds(pl.multiple_of(which[0] * size, BLK), size)
    store_coded(first, share_of(scaled[at, :], units[at, :], stats[...]))


def scaled_of(own, starts, owners, which, back, w, units, gains, inv, ranks, slots, parts):
    width = w.shape[1]
    pieces = 5
    size = DV // parts
    vmem = pl.BlockSpec(memory_space=pltpu.VMEM)
    return pl.pallas_call(
        functools.partial(scaled_kernel, ranks, slots, starts.shape[0]),
        in_specs=[smem()] * 4
        + [vmem, pl.BlockSpec(memory_space=pl.ANY), vmem, vmem, vmem],
        out_specs=(vmem, vmem, vmem),
        out_shape=(
            struct((DV, ROWS), F32),
            struct((BLK, ROWS), F32),
            struct((HEAD + size, ROWS), I16),
        ),
        scratch_shapes=[
            pltpu.VMEM(back.shape, F32),
            pltpu.VMEM((width, ROWS), BF16),
            pltpu.VMEM((pieces, DV // pieces, width), BF16),
            pltpu.SemaphoreType.DMA((pieces,)),
        ],
        compiler_params=params(36),
        cost_estimate=cost(2 * ROWS * DV * width, 2 * DV * width + 12 * ROWS * DV),
        name="scaled",
    )(own, starts, owners, which.reshape(1), back, w, units, gains, inv)


def chunks_kernel(which, scaled, units, stats, *outs):
    size = outs[0].shape[0]
    for k, out in enumerate(outs):
        at = pl.ds(pl.multiple_of(which[k] * size, BLK), size)
        out[...] = share_of(scaled[at, :], units[at, :], stats[...])


def chunks_of(which, scaled, units, stats, parts):
    vmem = pl.BlockSpec(memory_space=pltpu.VMEM)
    count = len(which)
    size = DV // parts
    return pl.pallas_call(
        chunks_kernel,
        in_specs=[smem(), vmem, vmem, vmem],
        out_specs=[vmem] * count,
        out_shape=[struct((size, ROWS), F32)] * count,
        compiler_params=params(),
        cost_estimate=cost(4 * count * size * ROWS, 12 * count * size * ROWS),
        name="chunks",
    )(jnp.stack(which), scaled, units, stats)


def code_kernel(share, out):
    store_coded(out, share[...])


def relay_kernel(share, came, out):
    store_coded(out, share[...] + decoded(came))


def finish_kernel(share, one, other, out):
    out[...] = (share[...] + decoded(one) + decoded(other)).astype(BF16)


def plain_call(kernel, name, kind, share, *extras):
    vmem = pl.BlockSpec(memory_space=pltpu.VMEM)
    size, lanes = share.shape
    return pl.pallas_call(
        kernel,
        in_specs=[vmem] * (1 + len(extras)),
        out_specs=vmem,
        out_shape=struct((size if kind == BF16 else HEAD + size, lanes), kind),
        compiler_params=params(),
        cost_estimate=cost(20 * size * lanes, 8 * size * lanes),
        name=name,
    )(share, *extras)


code = functools.partial(plain_call, code_kernel, "code", I16)
relay = functools.partial(plain_call, relay_kernel, "relay", I16)
finish = functools.partial(plain_call, finish_kernel, "finish", BF16)


def first_chunk(place, parts):
    last = parts - 1
    return jnp.where(place < 2, last, 0) if parts == 4 else jnp.full_like(place, last)


def scatter_sum(first, scaled, units, stats, place, parts):
    last = parts - 1
    if parts == 4:
        low = place < 2
        outer, inner = [(0, 1), (3, 2)], [(1, 2), (2, 1)]
        pairs = [(0, 1), (1, 0), (2, 3), (3, 2)]
        turn = place + 1 - 2 * (place % 2)
        a = lax.ppermute(first, "mp", outer)
        far, near, next_to, own = chunks_of(
            [jnp.where(low, 3, 0), jnp.where(low, 2, 1), turn, place], scaled, units, stats, parts
        )
        second = code(near)
        third = relay(far, a)
        c = lax.ppermute(third, "mp", inner)
        second, _ = lax.optimization_barrier((second, third))
        b = lax.ppermute(second, "mp", outer)
        fourth = relay(next_to, c)
        e = lax.ppermute(fourth, "mp", pairs)
        d = lax.ppermute(relay(near, b), "mp", inner)
        return finish(own, d, e)
    which = [jnp.zeros_like(place)]
    for s in range(1, last):
        which += [jnp.minimum(last - s + place, last), jnp.maximum(place - last + s, 0)]
    held = chunks_of(which + [place], scaled, units, stats, parts)
    up, down = first, code(held[0])
    for s in range(1, parts):
        up = lax.ppermute(up, "mp", [(z, z + 1) for z in range(s)])
        down = lax.ppermute(down, "mp", [(last - z, last - z - 1) for z in range(s)])
        if s < last:
            up, down = relay(held[2 * s - 1], up), relay(held[2 * s], down)
    return finish(held[-1], up, down)


def summed(values, parts):
    if parts & (parts - 1):
        return lax.psum(values, "mp")
    hop = 1
    while hop < parts:
        values = values + lax.ppermute(values, "mp", [(i, i ^ hop) for i in range(parts)])
        hop *= 2
    return values


def exchange(rows, ranks):
    shape = rows.shape
    split = rows.reshape(ranks, shape[0] // ranks, shape[1])
    return lax.all_to_all(split, "seq", split_axis=0, concat_axis=0, tiled=True).reshape(shape)


def body(
    vit_hidden,
    vit_gain,
    vit_bias,
    proj_weight,
    text_emb,
    llm_gain,
    cotangent,
    tile_start,
    tile_owner,
):
    ranks = lax.axis_size("seq")
    parts = lax.axis_size("mp")
    own_index = lax.axis_index("seq")
    place = lax.axis_index("mp")
    slots = -(-TILE_BLOCKS // ranks)
    width = proj_weight.shape[1]
    local_blocks = text_emb.shape[0] // BLK
    own = own_index.reshape(1)
    gain = llm_gain.reshape(1, width)

    sent = embed(own, tile_start, tile_owner, vit_hidden, vit_gain, vit_bias, proj_weight, ranks, slots)
    came = exchange(sent, ranks)

    global_block = (jnp.arange(local_blocks, dtype=I32) * ranks + own_index)[:, None]
    offset = global_block - tile_start[None, :]
    covered = (offset >= 0) & (offset < TILE_BLOCKS)
    slot_of = jnp.sum(
        jnp.where(covered, tile_owner[None, :] * slots + offset // ranks + 1, 0), axis=1
    ) - 1
    owners = jnp.arange(ranks, dtype=I32)[:, None]
    start_of = jnp.sum(jnp.where(tile_owner[None, :] == owners, tile_start[None, :], 0), axis=1)
    tile_block = (own_index - start_of[:, None]) % ranks + (
        jnp.arange(slots, dtype=I32)[None, :] * ranks
    )
    local_of = jnp.minimum((start_of[:, None] + tile_block) // ranks, local_blocks - 1)
    cot_blocks = cotangent.reshape(local_blocks, BLK, width)
    cot_image = jnp.take(cot_blocks, local_of.reshape(-1), axis=0, mode="clip")
    cot_image = cot_image.reshape(-1, width)

    text_part = text_sums(text_emb, cotangent, gain)

    sums = summed(image_sums(came, cot_image, gain, text_part), parts)
    back = exchange(image_grad(came, cot_image, gain, sums), ranks)
    normed, grad_text, after = outputs(slot_of, came, text_emb, cotangent, gain, sums)

    units, gains, inv = units_of(vit_hidden, vit_gain, after)
    scaled, stats, first = scaled_of(
        own, tile_start, tile_owner, first_chunk(place, parts), back, proj_weight, units, gains,
        inv, ranks, slots, parts
    )
    grad_vit = scatter_sum(first, scaled, units, stats, place, parts)
    return (normed, grad_text, grad_vit.T)


def solution(mesh):
    in_specs = (
        P("seq", None),
        P(),
        P(),
        P(None, "mp"),
        P("seq", "mp"),
        P("mp"),
        P("seq", "mp"),
        P(),
        P(),
    )
    out_specs = (P("seq", "mp"), P("seq", "mp"), P("seq", "mp"))
    return jax.shard_map(body, mesh=mesh, in_specs=in_specs, out_specs=out_specs, check_vma=False)
```

```python
import functools

import jax
import jax.numpy as jnp
from jax import lax
from jax.experimental import pallas as pl
from jax.experimental.pallas import tpu as pltpu
from jax.sharding import PartitionSpec as P

D = 8192
DV = 3200
BLK = 8
TILE_BLOCKS = 32
ROWS = TILE_BLOCKS * BLK
EPSILON = 1e-05
LANES = 128
HEAD = 16
FULL = 32767.0
STEPS_PER_OCTAVE = 16.0
LN2 = 0.6931471805599453
F32 = jnp.float32
BF16 = jnp.bfloat16
I32 = jnp.int32
I16 = jnp.int16


def struct(shape, kind):
    return jax.ShapeDtypeStruct(shape, kind)


def smem():
    return pl.BlockSpec(memory_space=pltpu.SMEM)


def params(mib=16):
    return pltpu.CompilerParams(vmem_limit_bytes=mib << 20)


def cost(flops, moved):
    return pl.CostEstimate(flops=int(flops), bytes_accessed=int(moved), transcendentals=0)


def column(row):
    return jnp.transpose(jnp.broadcast_to(row, (LANES, row.shape[1])))


def as_row(col):
    return jnp.transpose(jnp.broadcast_to(col, (col.shape[0], LANES)))


def own_start_of(own, starts, owners, tiles):
    found = starts[0]
    for t in range(1, tiles):
        found = jnp.where(owners[t] == own, starts[t], found)
    return found


def norm_stats(values):
    mean = jnp.mean(values, axis=1, keepdims=True)
    centred = values - mean
    inv_std = lax.rsqrt(jnp.mean(centred * centred, axis=1, keepdims=True) + EPSILON)
    return mean, centred, inv_std


def embed_kernel(
    ranks, slots, tiles, own, starts, owners, x, vg, vb, w, out, natural, ordered, held, made, sems
):
    pieces = held.shape[0]
    tile = held.shape[2]
    coming = [
        pltpu.make_async_copy(w.at[:, i * tile : (i + 1) * tile], held.at[i], sems.at[i])
        for i in range(pieces)
    ]
    for copy in coming:
        copy.start()
    start = own_start_of(own[0], starts, owners, tiles)
    gain, bias = vg[...].reshape(1, DV), vb[...].reshape(1, DV)
    for c in range(0, ROWS, 64):
        _, centred, inv_std = norm_stats(x[c : c + 64, :].astype(F32))
        normed = (centred * inv_std * gain + bias).astype(BF16)
        natural[c : c + 64, :] = normed.astype(F32)
    for p in range(0, ranks * slots, 2):
        pair = []
        for q in (p, p + 1):
            block = lax.rem(q // slots - start + ranks * 1024, ranks) + (q % slots) * ranks
            block = jnp.minimum(block, TILE_BLOCKS - 1)
            pair.append(natural[pl.ds(pl.multiple_of(block * BLK, BLK), BLK), :])
        ordered[p * BLK : (p + 2) * BLK, :] = jnp.concatenate(pair, axis=0).astype(BF16)
    going = []
    for i in range(pieces):
        coming[i].wait()
        made[i, :, :] = jnp.dot(ordered[...], held[i], preferred_element_type=F32).astype(BF16)
        going.append(
            pltpu.make_async_copy(
                made.at[i], out.at[:, i * tile : (i + 1) * tile], sems.at[pieces + i]
            )
        )
        going[i].start()
    for copy in going:
        copy.wait()


def embed(own, starts, owners, x, vg, vb, w, ranks, slots):
    width = w.shape[1]
    pieces = 4
    tile = width // pieces
    rows = ranks * slots * BLK
    vmem = pl.BlockSpec(memory_space=pltpu.VMEM)
    anywhere = pl.BlockSpec(memory_space=pl.ANY)
    return pl.pallas_call(
        functools.partial(embed_kernel, ranks, slots, starts.shape[0]),
        in_specs=[smem(), smem(), smem(), vmem, vmem, vmem, anywhere],
        out_specs=anywhere,
        out_shape=struct((rows, width), BF16),
        scratch_shapes=[
            pltpu.VMEM((ROWS, DV), F32),
            pltpu.VMEM((rows, DV), BF16),
            pltpu.VMEM((pieces, DV, tile), BF16),
            pltpu.VMEM((pieces, rows, tile), BF16),
            pltpu.SemaphoreType.DMA((2 * pieces,)),
        ],
        compiler_params=params(63),
        cost_estimate=cost(2 * rows * DV * width, 2 * DV * width + 4 * ROWS * DV),
        name="embed",
    )(own, starts, owners, x, vg, vb, w)


def turned_kernel(x, vg, after, xt, gains, stats):
    mean, _, inv_std = norm_stats(x[...].astype(F32))
    mean, inv_std = as_row(mean)[:BLK, :], as_row(inv_std)[:BLK, :]
    first = lax.broadcasted_iota(I32, mean.shape, 0) == 0
    stats[...] = jnp.where(first, mean, inv_std)
    gain = vg[...].reshape(1, DV)
    for c in range(0, DV, 640):
        xt[c : c + 640, :] = jnp.transpose(x[:, c : c + 640].astype(F32)).astype(BF16)
        gains[c : c + 640, :] = column(gain[:, c : c + 640])


def turned_of(x, vg, after):
    return pl.pallas_call(
        turned_kernel,
        out_shape=(struct((DV, ROWS), BF16), struct((DV, LANES), F32), struct((BLK, ROWS), F32)),
        compiler_params=params(32),
        cost_estimate=cost(10 * ROWS * DV, 8 * ROWS * DV),
        name="turned",
    )(x, vg, after)


def sums_of(m, gc):
    squares = as_row(jnp.sum(m * m, axis=1, keepdims=True))[:BLK, :]
    products = as_row(jnp.sum(gc * m, axis=1, keepdims=True))[:BLK, :]
    first = lax.broadcasted_iota(I32, squares.shape, 0) == 0
    return jnp.where(first, squares, products)


def text_sums_kernel(text, cot, gain, out):
    out[...] = sums_of(text[...].astype(F32), gain[...] * cot[...].astype(F32))


def text_sums(text, cot, gain):
    rows, width = text.shape
    step = lambda i: (i, 0)
    return pl.pallas_call(
        text_sums_kernel,
        grid=(rows // LANES,),
        in_specs=[
            pl.BlockSpec((LANES, width), step),
            pl.BlockSpec((LANES, width), step),
            pl.BlockSpec((1, width), lambda i: (0, 0)),
        ],
        out_specs=pl.BlockSpec((BLK, LANES), lambda i: (0, i)),
        out_shape=struct((BLK, rows), F32),
        compiler_params=params(),
        cost_estimate=cost(6 * rows * width, 4 * rows * width),
        name="text_sums",
    )(text, cot, gain)


def image_sums_kernel(image, m, cot, gain, text, out):
    i = pl.program_id(0)

    @pl.when(i == 0)
    def _():
        out[:, image:] = text[...]

    found = sums_of(m[...].astype(F32), gain[...] * cot[...].astype(F32))
    out[:, pl.ds(pl.multiple_of(i * LANES, LANES), LANES)] = found


def image_sums(m, cot, gain, text):
    rows, width = m.shape
    total = rows + text.shape[1]
    step = lambda i: (i, 0)
    whole = lambda i: (0, 0)
    return pl.pallas_call(
        functools.partial(image_sums_kernel, rows),
        grid=(rows // LANES,),
        in_specs=[
            pl.BlockSpec((LANES, width), step),
            pl.BlockSpec((LANES, width), step),
            pl.BlockSpec((1, width), whole),
            pl.BlockSpec((BLK, text.shape[1]), whole),
        ],
        out_specs=pl.BlockSpec((BLK, total), whole),
        out_shape=struct((BLK, total), F32),
        compiler_params=params(),
        cost_estimate=cost(6 * rows * width, 4 * rows * width),
        name="image_sums",
    )(m, cot, gain, text)


def row_factors(sums):
    inv_rms = lax.rsqrt(sums[0:1, :] / D + EPSILON)
    return inv_rms, inv_rms * inv_rms * inv_rms * sums[1:2, :] / D


def image_grad_kernel(m, cot, gain, sums, out):
    inv_rms, factor = row_factors(sums[...])
    inv_rms, factor = column(inv_rms)[:, :1], column(factor)[:, :1]
    grad_gain = gain[...] * cot[...].astype(F32)
    out[...] = (inv_rms * grad_gain - m[...].astype(F32) * factor).astype(BF16)


def image_grad(m, cot, gain, sums):
    rows, width = m.shape
    step = lambda i: (i, 0)
    return pl.pallas_call(
        image_grad_kernel,
        grid=(rows // LANES,),
        in_specs=[
            pl.BlockSpec((LANES, width), step),
            pl.BlockSpec((LANES, width), step),
            pl.BlockSpec((1, width), lambda i: (0, 0)),
            pl.BlockSpec((BLK, LANES), lambda i: (0, i)),
        ],
        out_specs=pl.BlockSpec((LANES, width), step),
        out_shape=pltpu.HBM((rows, width), BF16),
        compiler_params=params(),
        cost_estimate=cost(6 * rows * width, 6 * rows * width),
        name="image_grad",
    )(m, cot, gain, sums)


def outputs_kernel(
    chunk, slot_of, m, text, cot, gain, sums, normed, grad, token, held, inv_col, fac_col
):
    i = pl.program_id(0)

    @pl.when(i == 0)
    def _():
        held[...] = m[...].astype(F32)
        token[...] = jnp.zeros_like(token)
        inv_rms, factor = row_factors(sums[...])
        inv_col[...] = column(inv_rms)
        fac_col[...] = column(factor)

    image = m.shape[0]
    words = text[...].astype(F32)
    grads = cot[...].astype(F32) * gain[...]
    for b in range(0, chunk, 2):
        normed_pair, grad_pair = [], []
        for c in (b, b + 1):
            local = i * chunk + c
            slot = slot_of[local]
            inside = slot >= 0
            at = pl.multiple_of(jnp.maximum(slot, 0) * BLK, BLK)
            row = pl.multiple_of(jnp.where(inside, at, image + local * BLK), BLK)
            inv_rms = inv_col[pl.ds(row, BLK), :][:, :1]
            factor = fac_col[pl.ds(row, BLK), :][:, :1]
            own = words[c * BLK : (c + 1) * BLK, :]
            merged = jnp.where(inside, held[pl.ds(at, BLK), :], own)
            slope = inv_rms * grads[c * BLK : (c + 1) * BLK, :] - merged * factor
            normed_pair.append(merged * inv_rms * gain[...])
            grad_pair.append(jnp.where(inside, 0.0, slope))
        rows = slice(b * BLK, (b + 2) * BLK)
        normed[rows, :] = jnp.concatenate(normed_pair, axis=0).astype(BF16)
        grad[rows, :] = jnp.concatenate(grad_pair, axis=0).astype(BF16)


def outputs(slot_of, m, text, cot, gain, sums):
    rows, width = text.shape
    chunk = 8
    step = lambda i: (i, 0)
    whole = lambda i: (0, 0)
    part = pl.BlockSpec((chunk * BLK, width), step)
    return pl.pallas_call(
        functools.partial(outputs_kernel, chunk),
        grid=(rows // (chunk * BLK),),
        in_specs=[
            smem(),
            pl.BlockSpec(m.shape, whole),
            part,
            part,
            pl.BlockSpec((1, width), whole),
            pl.BlockSpec(sums.shape, whole),
        ],
        out_specs=(part, part, pl.BlockSpec((BLK, LANES), whole)),
        out_shape=(
            struct((rows, width), BF16),
            struct((rows, width), BF16),
            struct((BLK, LANES), F32),
        ),
        scratch_shapes=[
            pltpu.VMEM(m.shape, F32),
            pltpu.VMEM((sums.shape[1], LANES), F32),
            pltpu.VMEM((sums.shape[1], LANES), F32),
        ],
        compiler_params=params(24),
        cost_estimate=cost(10 * rows * width, 9 * rows * width),
        name="outputs",
    )(slot_of, m, text, cot, gain, sums)


def coded(values):
    most = jnp.maximum(jnp.max(jnp.abs(values), axis=0, keepdims=True), 2.0**-100)
    code = jnp.floor(jnp.log(most) * (STEPS_PER_OCTAVE / LN2)) + 2.0
    inverse = FULL / jnp.exp(code * (LN2 / STEPS_PER_OCTAVE))
    scaled = jnp.clip(jnp.floor(values * inverse + 0.5), -FULL, FULL)
    head = jnp.broadcast_to(code, (HEAD, values.shape[1]))
    return head.astype(I32).astype(I16), scaled.astype(I32).astype(I16)


def store_coded(ref, values):
    head, body = coded(values)
    ref[:HEAD, :] = head
    ref[HEAD:, :] = body


def decoded(ref):
    code = ref[:HEAD, :].astype(I32).astype(F32)[:1, :]
    scale = jnp.exp(code * (LN2 / STEPS_PER_OCTAVE)) / FULL
    return ref[HEAD:, :].astype(I32).astype(F32) * scale


def unit_of(x, mean, inv_std):
    return (x.astype(F32) - mean) * inv_std


def share_of(scaled, x, stats):
    mean, slope, scale = stats[0:1, :], stats[1:2, :], stats[3:4, :]
    return scale * (scaled - mean - unit_of(x, stats[2:3, :], scale) * slope)


def scaled_kernel(
    ranks, slots, tiles, own, starts, owners, which, back, w, xt, gains, inv,
    out, stats, first, wide, grad_t, scaled, held, sems
):
    pieces, tile = held.shape[0], held.shape[1]
    coming = [
        pltpu.make_async_copy(w.at[i * tile : (i + 1) * tile, :], held.at[i], sems.at[i])
        for i in range(pieces)
    ]
    for copy in coming:
        copy.start()
    start = own_start_of(own[0], starts, owners, tiles)
    wide[...] = back[...].astype(F32)
    for b in range(0, TILE_BLOCKS, 16):
        group = []
        for q in range(b, b + 16):
            slot = lax.rem(start + q, ranks) * slots + q // ranks
            group.append(wide[pl.ds(pl.multiple_of(slot * BLK, BLK), BLK), :])
        rows = jnp.concatenate(group, axis=0)
        grad_t[:, b * BLK : (b + 16) * BLK] = jnp.transpose(rows).astype(BF16)
    total = jnp.zeros((1, ROWS), F32)
    along = jnp.zeros((1, ROWS), F32)
    going = []
    mean, scale = inv[0:1, :], inv[1:2, :]
    for i in range(pieces):
        coming[i].wait()
        at = slice(i * tile, (i + 1) * tile)
        part = jnp.dot(held[i], grad_t[...], preferred_element_type=F32)
        s = part * jnp.concatenate([gains[at, :], gains[at, :]], axis=1)
        scaled[at, :] = s
        going.append(pltpu.make_async_copy(scaled.at[at, :], out.at[at, :], sems.at[pieces + i]))
        going[i].start()
        total = total + jnp.sum(s, axis=0, keepdims=True)
        along = along + jnp.sum(s * unit_of(xt[at, :], mean, scale), axis=0, keepdims=True)
    rest = jnp.zeros((BLK - 4, ROWS), F32)
    stats[...] = jnp.concatenate([total / DV, along / DV, mean, scale, rest], axis=0)
    size = first.shape[0] - HEAD
    at = pl.ds(pl.multiple_of(which[0] * size, BLK), size)
    store_coded(first, share_of(scaled[at, :], xt[at, :], stats[...]))
    for copy in going:
        copy.wait()


def scaled_of(own, starts, owners, which, back, w, xt, gains, inv, ranks, slots, parts):
    width = w.shape[1]
    size = DV // parts
    pieces = 5
    vmem = pl.BlockSpec(memory_space=pltpu.VMEM)
    return pl.pallas_call(
        functools.partial(scaled_kernel, ranks, slots, starts.shape[0]),
        in_specs=[smem()] * 4 + [vmem, pl.BlockSpec(memory_space=pl.ANY), vmem, vmem, vmem],
        out_specs=(pl.BlockSpec(memory_space=pltpu.HBM), vmem, vmem),
        out_shape=(
            pltpu.HBM((DV, ROWS), F32),
            struct((BLK, ROWS), F32),
            struct((HEAD + size, ROWS), I16),
        ),
        scratch_shapes=[
            pltpu.VMEM(back.shape, F32),
            pltpu.VMEM((width, ROWS), BF16),
            pltpu.VMEM((DV, ROWS), F32),
            pltpu.VMEM((pieces, DV // pieces, width), BF16),
            pltpu.SemaphoreType.DMA((2 * pieces,)),
        ],
        compiler_params=params(36),
        cost_estimate=cost(2 * ROWS * DV * width, 2 * DV * width + 12 * ROWS * DV),
        name="scaled",
    )(own, starts, owners, which.reshape(1), back, w, xt, gains, inv)


def chunks_kernel(which, scaled, xt, stats, *outs):
    size = outs[0].shape[0]
    for k, out in enumerate(outs):
        at = pl.ds(pl.multiple_of(which[k] * size, BLK), size)
        out[...] = share_of(scaled[at, :], xt[at, :], stats[...])


def chunks_of(which, scaled, xt, stats, parts):
    vmem = pl.BlockSpec(memory_space=pltpu.VMEM)
    count = len(which)
    size = DV // parts
    return pl.pallas_call(
        chunks_kernel,
        in_specs=[smem(), vmem, vmem, vmem],
        out_specs=[vmem] * count,
        out_shape=[struct((size, ROWS), F32)] * count,
        compiler_params=params(),
        cost_estimate=cost(4 * count * size * ROWS, 12 * count * size * ROWS),
        name="chunks",
    )(jnp.stack(which), scaled, xt, stats)


def code_kernel(share, out):
    store_coded(out, share[...])


def relay_kernel(share, came, valid, out):
    store_coded(out, share[...] + jnp.where(valid[0] > 0, decoded(came), 0.0))


def finish_kernel(share, one, other, valid, out):
    total = share[...] + jnp.where(valid[0] > 0, decoded(one), 0.0) + decoded(other)
    out[...] = total.astype(BF16)


def plain_call(kernel, name, kind, share, *extras):
    vmem = pl.BlockSpec(memory_space=pltpu.VMEM)
    size, lanes = share.shape
    return pl.pallas_call(
        kernel,
        in_specs=[vmem] * len(extras) + ([smem()] if extras else [vmem]),
        out_specs=vmem,
        out_shape=struct((size if kind == BF16 else HEAD + size, lanes), kind),
        compiler_params=params(),
        cost_estimate=cost(20 * size * lanes, 8 * size * lanes),
        name=name,
    )(share, *extras)


code = functools.partial(plain_call, code_kernel, "code", I16)
relay = functools.partial(plain_call, relay_kernel, "relay", I16)
finish = functools.partial(plain_call, finish_kernel, "finish", BF16)


def first_chunk(place, parts):
    last = parts - 1
    return jnp.where(place < 2, last, 0) if parts == 4 else jnp.full_like(place, last)


def scatter_sum(first, scaled, xt, stats, place, parts):
    last = parts - 1
    if parts == 4:
        low = place < 2
        outer, inner = [(0, 1), (1, 0), (2, 3), (3, 2)], [(0, 0), (1, 2), (2, 1), (3, 3)]
        middle = ((place == 1) | (place == 2)).astype(I32).reshape(1)
        always = jnp.ones((1,), I32)
        turn = place + 1 - 2 * (place % 2)
        a = lax.ppermute(first, "mp", outer)
        far, near, next_to, own = chunks_of(
            [jnp.where(low, 3, 0), jnp.where(low, 2, 1), turn, place], scaled, xt, stats, parts
        )
        second = code(near)
        third = relay(far, a, always)
        c = lax.ppermute(third, "mp", inner)
        second, _ = lax.optimization_barrier((second, third))
        b = lax.ppermute(second, "mp", outer)
        fourth = relay(next_to, c, middle)
        e = lax.ppermute(fourth, "mp", outer)
        d = lax.ppermute(relay(near, b, always), "mp", inner)
        return finish(own, d, e, middle)
    which = [jnp.zeros_like(place)]
    for s in range(1, last):
        which += [jnp.minimum(last - s + place, last), jnp.maximum(place - last + s, 0)]
    held = chunks_of(which + [place], scaled, xt, stats, parts)
    up, down = first, code(held[0])
    always = jnp.ones((1,), I32)
    for s in range(1, parts):
        up = lax.ppermute(up, "mp", [(z, z + 1) for z in range(s)])
        down = lax.ppermute(down, "mp", [(last - z, last - z - 1) for z in range(s)])
        if s < last:
            up, down = relay(held[2 * s - 1], up, always), relay(held[2 * s], down, always)
    return finish(held[-1], up, down, always)


def summed(values, parts):
    if parts & (parts - 1):
        return lax.psum(values, "mp")
    hop = 1
    while hop < parts:
        values = values + lax.ppermute(values, "mp", [(i, i ^ hop) for i in range(parts)])
        hop *= 2
    return values


def exchange(rows, ranks):
    shape = rows.shape
    split = rows.reshape(ranks, shape[0] // ranks, shape[1])
    return lax.all_to_all(split, "seq", split_axis=0, concat_axis=0, tiled=True).reshape(shape)


def body(
    vit_hidden,
    vit_gain,
    vit_bias,
    proj_weight,
    text_emb,
    llm_gain,
    cotangent,
    tile_start,
    tile_owner,
):
    ranks = lax.axis_size("seq")
    parts = lax.axis_size("mp")
    own_index = lax.axis_index("seq")
    place = lax.axis_index("mp")
    slots = -(-TILE_BLOCKS // ranks)
    width = proj_weight.shape[1]
    local_blocks = text_emb.shape[0] // BLK
    own = own_index.reshape(1)
    gain = llm_gain.reshape(1, width)

    sent = embed(own, tile_start, tile_owner, vit_hidden, vit_gain, vit_bias, proj_weight, ranks, slots)
    came = exchange(sent, ranks)

    global_block = (jnp.arange(local_blocks, dtype=I32) * ranks + own_index)[:, None]
    offset = global_block - tile_start[None, :]
    covered = (offset >= 0) & (offset < TILE_BLOCKS)
    slot_of = jnp.sum(
        jnp.where(covered, tile_owner[None, :] * slots + offset // ranks + 1, 0), axis=1
    ) - 1
    owners = jnp.arange(ranks, dtype=I32)[:, None]
    start_of = jnp.sum(jnp.where(tile_owner[None, :] == owners, tile_start[None, :], 0), axis=1)
    tile_block = (own_index - start_of[:, None]) % ranks + (
        jnp.arange(slots, dtype=I32)[None, :] * ranks
    )
    local_of = jnp.minimum((start_of[:, None] + tile_block) // ranks, local_blocks - 1)
    cot_blocks = cotangent.reshape(local_blocks, BLK, width)
    cot_image = jnp.take(cot_blocks, local_of.reshape(-1), axis=0, mode="clip")
    cot_image = cot_image.reshape(-1, width)

    text_part = text_sums(text_emb, cotangent, gain)

    sums = summed(image_sums(came, cot_image, gain, text_part), parts)
    back = exchange(image_grad(came, cot_image, gain, sums), ranks)
    normed, grad_text, after = outputs(slot_of, came, text_emb, cotangent, gain, sums)

    xt, gains, row_stats = turned_of(vit_hidden, vit_gain, after)
    scaled, stats, first = scaled_of(
        own, tile_start, tile_owner, first_chunk(place, parts), back, proj_weight, xt, gains,
        row_stats, ranks, slots, parts
    )
    grad_vit = scatter_sum(first, scaled, xt, stats, place, parts)
    return (normed, grad_text, grad_vit.T)


def solution(mesh):
    in_specs = (
        P("seq", None),
        P(),
        P(),
        P(None, "mp"),
        P("seq", "mp"),
        P("mp"),
        P("seq", "mp"),
        P(),
        P(),
    )
    out_specs = (P("seq", "mp"), P("seq", "mp"), P("seq", "mp"))
    return jax.shard_map(body, mesh=mesh, in_specs=in_specs, out_specs=out_specs, check_vma=False)
```

```python
import functools

import jax
import jax.numpy as jnp
from jax import lax
from jax.experimental import pallas as pl
from jax.experimental.pallas import tpu as pltpu
from jax.sharding import PartitionSpec as P

D = 8192
DV = 3200
BLK = 8
TILE_BLOCKS = 32
ROWS = TILE_BLOCKS * BLK
EPSILON = 1e-05
LANES = 128
HEAD = 16
FULL = 32767.0
STEPS_PER_OCTAVE = 16.0
LN2 = 0.6931471805599453
F32 = jnp.float32
BF16 = jnp.bfloat16
I32 = jnp.int32
I16 = jnp.int16


def struct(shape, kind):
    return jax.ShapeDtypeStruct(shape, kind)


def smem():
    return pl.BlockSpec(memory_space=pltpu.SMEM)


def params(mib=16):
    return pltpu.CompilerParams(vmem_limit_bytes=mib << 20)


def cost(flops, moved):
    return pl.CostEstimate(flops=int(flops), bytes_accessed=int(moved), transcendentals=0)


def column(row):
    return jnp.transpose(jnp.broadcast_to(row, (LANES, row.shape[1])))


def as_row(col):
    return jnp.transpose(jnp.broadcast_to(col, (col.shape[0], LANES)))


def own_start_of(own, starts, owners, tiles):
    found = starts[0]
    for t in range(1, tiles):
        found = jnp.where(owners[t] == own, starts[t], found)
    return found


def norm_stats(values):
    mean = jnp.mean(values, axis=1, keepdims=True)
    centred = values - mean
    inv_std = lax.rsqrt(jnp.mean(centred * centred, axis=1, keepdims=True) + EPSILON)
    return mean, centred, inv_std


def embed_kernel(
    ranks, slots, tiles, own, starts, owners, x, vg, vb, w, out, natural, ordered, held, made, sems
):
    pieces = held.shape[0]
    tile = held.shape[2]
    coming = [
        pltpu.make_async_copy(w.at[:, i * tile : (i + 1) * tile], held.at[i], sems.at[i])
        for i in range(pieces)
    ]
    for copy in coming:
        copy.start()
    start = own_start_of(own[0], starts, owners, tiles)
    gain, bias = vg[...].reshape(1, DV), vb[...].reshape(1, DV)
    for c in range(0, ROWS, 64):
        _, centred, inv_std = norm_stats(x[c : c + 64, :].astype(F32))
        normed = (centred * inv_std * gain + bias).astype(BF16)
        natural[c : c + 64, :] = normed.astype(F32)
    for p in range(0, ranks * slots, 2):
        pair = []
        for q in (p, p + 1):
            block = lax.rem(q // slots - start + ranks * 1024, ranks) + (q % slots) * ranks
            block = jnp.minimum(block, TILE_BLOCKS - 1)
            pair.append(natural[pl.ds(pl.multiple_of(block * BLK, BLK), BLK), :])
        ordered[p * BLK : (p + 2) * BLK, :] = jnp.concatenate(pair, axis=0).astype(BF16)
    going = []
    for i in range(pieces):
        coming[i].wait()
        made[i, :, :] = jnp.dot(ordered[...], held[i], preferred_element_type=F32).astype(BF16)
        going.append(
            pltpu.make_async_copy(
                made.at[i], out.at[:, i * tile : (i + 1) * tile], sems.at[pieces + i]
            )
        )
        going[i].start()
    for copy in going:
        copy.wait()


def embed(own, starts, owners, x, vg, vb, w, ranks, slots):
    width = w.shape[1]
    pieces = 4
    tile = width // pieces
    rows = ranks * slots * BLK
    vmem = pl.BlockSpec(memory_space=pltpu.VMEM)
    anywhere = pl.BlockSpec(memory_space=pl.ANY)
    return pl.pallas_call(
        functools.partial(embed_kernel, ranks, slots, starts.shape[0]),
        in_specs=[smem(), smem(), smem(), vmem, vmem, vmem, anywhere],
        out_specs=anywhere,
        out_shape=struct((rows, width), BF16),
        scratch_shapes=[
            pltpu.VMEM((ROWS, DV), F32),
            pltpu.VMEM((rows, DV), BF16),
            pltpu.VMEM((pieces, DV, tile), BF16),
            pltpu.VMEM((pieces, rows, tile), BF16),
            pltpu.SemaphoreType.DMA((2 * pieces,)),
        ],
        compiler_params=params(63),
        cost_estimate=cost(2 * rows * DV * width, 2 * DV * width + 4 * ROWS * DV),
        name="embed",
    )(own, starts, owners, x, vg, vb, w)


def turned_kernel(x, vg, after, xt, gains, stats):
    mean, _, inv_std = norm_stats(x[...].astype(F32))
    mean, inv_std = as_row(mean)[:BLK, :], as_row(inv_std)[:BLK, :]
    first = lax.broadcasted_iota(I32, mean.shape, 0) == 0
    stats[...] = jnp.where(first, mean, inv_std)
    gain = vg[...].reshape(1, DV)
    for c in range(0, DV, 640):
        xt[c : c + 640, :] = jnp.transpose(x[:, c : c + 640].astype(F32)).astype(BF16)
        gains[c : c + 640, :] = column(gain[:, c : c + 640])


def turned_of(x, vg, after):
    return pl.pallas_call(
        turned_kernel,
        out_shape=(struct((DV, ROWS), BF16), struct((DV, LANES), F32), struct((BLK, ROWS), F32)),
        compiler_params=params(32),
        cost_estimate=cost(10 * ROWS * DV, 8 * ROWS * DV),
        name="turned",
    )(x, vg, after)


def sums_of(m, gc):
    squares = as_row(jnp.sum(m * m, axis=1, keepdims=True))[:BLK, :]
    products = as_row(jnp.sum(gc * m, axis=1, keepdims=True))[:BLK, :]
    first = lax.broadcasted_iota(I32, squares.shape, 0) == 0
    return jnp.where(first, squares, products)


def text_sums_kernel(text, cot, gain, out):
    out[...] = sums_of(text[...].astype(F32), gain[...] * cot[...].astype(F32))


def text_sums(text, cot, gain):
    rows, width = text.shape
    step = lambda i: (i, 0)
    return pl.pallas_call(
        text_sums_kernel,
        grid=(rows // LANES,),
        in_specs=[
            pl.BlockSpec((LANES, width), step),
            pl.BlockSpec((LANES, width), step),
            pl.BlockSpec((1, width), lambda i: (0, 0)),
        ],
        out_specs=pl.BlockSpec((BLK, LANES), lambda i: (0, i)),
        out_shape=struct((BLK, rows), F32),
        compiler_params=params(),
        cost_estimate=cost(6 * rows * width, 4 * rows * width),
        name="text_sums",
    )(text, cot, gain)


def image_sums_kernel(image, m, cot, gain, text, out):
    i = pl.program_id(0)

    @pl.when(i == 0)
    def _():
        out[:, image:] = text[...]

    found = sums_of(m[...].astype(F32), gain[...] * cot[...].astype(F32))
    out[:, pl.ds(pl.multiple_of(i * LANES, LANES), LANES)] = found


def image_sums(m, cot, gain, text):
    rows, width = m.shape
    total = rows + text.shape[1]
    step = lambda i: (i, 0)
    whole = lambda i: (0, 0)
    return pl.pallas_call(
        functools.partial(image_sums_kernel, rows),
        grid=(rows // LANES,),
        in_specs=[
            pl.BlockSpec((LANES, width), step),
            pl.BlockSpec((LANES, width), step),
            pl.BlockSpec((1, width), whole),
            pl.BlockSpec((BLK, text.shape[1]), whole),
        ],
        out_specs=pl.BlockSpec((BLK, total), whole),
        out_shape=struct((BLK, total), F32),
        compiler_params=params(),
        cost_estimate=cost(6 * rows * width, 4 * rows * width),
        name="image_sums",
    )(m, cot, gain, text)


def row_factors(sums):
    inv_rms = lax.rsqrt(sums[0:1, :] / D + EPSILON)
    return inv_rms, inv_rms * inv_rms * inv_rms * sums[1:2, :] / D


def image_grad_kernel(m, cot, gain, sums, out):
    inv_rms, factor = row_factors(sums[...])
    inv_rms, factor = column(inv_rms)[:, :1], column(factor)[:, :1]
    grad_gain = gain[...] * cot[...].astype(F32)
    out[...] = (inv_rms * grad_gain - m[...].astype(F32) * factor).astype(BF16)


def image_grad(m, cot, gain, sums):
    rows, width = m.shape
    step = lambda i: (i, 0)
    return pl.pallas_call(
        image_grad_kernel,
        grid=(rows // LANES,),
        in_specs=[
            pl.BlockSpec((LANES, width), step),
            pl.BlockSpec((LANES, width), step),
            pl.BlockSpec((1, width), lambda i: (0, 0)),
            pl.BlockSpec((BLK, LANES), lambda i: (0, i)),
        ],
        out_specs=pl.BlockSpec((LANES, width), step),
        out_shape=pltpu.HBM((rows, width), BF16),
        compiler_params=params(),
        cost_estimate=cost(6 * rows * width, 6 * rows * width),
        name="image_grad",
    )(m, cot, gain, sums)


def outputs_kernel(
    chunk, slot_of, m, text, cot, gain, sums, normed, grad, token, held, inv_col, fac_col
):
    i = pl.program_id(0)

    @pl.when(i == 0)
    def _():
        held[...] = m[...].astype(F32)
        token[...] = jnp.zeros_like(token)
        inv_rms, factor = row_factors(sums[...])
        inv_col[...] = column(inv_rms)
        fac_col[...] = column(factor)

    image = m.shape[0]
    words = text[...].astype(F32)
    grads = cot[...].astype(F32) * gain[...]
    for b in range(0, chunk, 2):
        normed_pair, grad_pair = [], []
        for c in (b, b + 1):
            local = i * chunk + c
            slot = slot_of[local]
            inside = slot >= 0
            at = pl.multiple_of(jnp.maximum(slot, 0) * BLK, BLK)
            row = pl.multiple_of(jnp.where(inside, at, image + local * BLK), BLK)
            inv_rms = inv_col[pl.ds(row, BLK), :][:, :1]
            factor = fac_col[pl.ds(row, BLK), :][:, :1]
            own = words[c * BLK : (c + 1) * BLK, :]
            merged = jnp.where(inside, held[pl.ds(at, BLK), :], own)
            slope = inv_rms * grads[c * BLK : (c + 1) * BLK, :] - merged * factor
            normed_pair.append(merged * inv_rms * gain[...])
            grad_pair.append(jnp.where(inside, 0.0, slope))
        rows = slice(b * BLK, (b + 2) * BLK)
        normed[rows, :] = jnp.concatenate(normed_pair, axis=0).astype(BF16)
        grad[rows, :] = jnp.concatenate(grad_pair, axis=0).astype(BF16)


def outputs(slot_of, m, text, cot, gain, sums):
    rows, width = text.shape
    chunk = 8
    step = lambda i: (i, 0)
    whole = lambda i: (0, 0)
    part = pl.BlockSpec((chunk * BLK, width), step)
    return pl.pallas_call(
        functools.partial(outputs_kernel, chunk),
        grid=(rows // (chunk * BLK),),
        in_specs=[
            smem(),
            pl.BlockSpec(m.shape, whole),
            part,
            part,
            pl.BlockSpec((1, width), whole),
            pl.BlockSpec(sums.shape, whole),
        ],
        out_specs=(part, part, pl.BlockSpec((BLK, LANES), whole)),
        out_shape=(
            struct((rows, width), BF16),
            struct((rows, width), BF16),
            struct((BLK, LANES), F32),
        ),
        scratch_shapes=[
            pltpu.VMEM(m.shape, F32),
            pltpu.VMEM((sums.shape[1], LANES), F32),
            pltpu.VMEM((sums.shape[1], LANES), F32),
        ],
        compiler_params=params(24),
        cost_estimate=cost(10 * rows * width, 9 * rows * width),
        name="outputs",
    )(slot_of, m, text, cot, gain, sums)


def coded(values):
    most = jnp.maximum(jnp.max(jnp.abs(values), axis=0, keepdims=True), 2.0**-100)
    code = jnp.floor(jnp.log(most) * (STEPS_PER_OCTAVE / LN2)) + 2.0
    inverse = FULL / jnp.exp(code * (LN2 / STEPS_PER_OCTAVE))
    scaled = jnp.clip(jnp.floor(values * inverse + 0.5), -FULL, FULL)
    head = jnp.broadcast_to(code, (HEAD, values.shape[1]))
    return head.astype(I32).astype(I16), scaled.astype(I32).astype(I16)


def store_coded(ref, values):
    head, body = coded(values)
    ref[:HEAD, :] = head
    ref[HEAD:, :] = body


def decoded(ref):
    code = ref[:HEAD, :].astype(I32).astype(F32)[:1, :]
    scale = jnp.exp(code * (LN2 / STEPS_PER_OCTAVE)) / FULL
    return ref[HEAD:, :].astype(I32).astype(F32) * scale


def unit_of(x, mean, inv_std):
    return (x.astype(F32) - mean) * inv_std


def share_of(scaled, x, stats):
    mean, slope, scale = stats[0:1, :], stats[1:2, :], stats[3:4, :]
    return scale * (scaled - mean - unit_of(x, stats[2:3, :], scale) * slope)


def scaled_kernel(
    ranks, slots, tiles, own, starts, owners, which, back, w, xt, gains, inv,
    out, stats, first, natural, grad_t, scaled, held, sems
):
    pieces, tile = held.shape[0], held.shape[1]
    coming = [
        pltpu.make_async_copy(w.at[i * tile : (i + 1) * tile, :], held.at[i], sems.at[i])
        for i in range(pieces)
    ]
    for copy in coming:
        copy.start()
    start = own_start_of(own[0], starts, owners, tiles)
    for q in range(TILE_BLOCKS):
        slot = lax.rem(start + q, ranks) * slots + q // ranks
        natural[q * BLK : (q + 1) * BLK, :] = back[pl.ds(pl.multiple_of(slot * BLK, BLK), BLK), :]
    grad_t[...] = jnp.transpose(natural[...])
    total = jnp.zeros((1, ROWS), F32)
    along = jnp.zeros((1, ROWS), F32)
    going = []
    mean, scale = inv[0:1, :], inv[1:2, :]
    for i in range(pieces):
        coming[i].wait()
        at = slice(i * tile, (i + 1) * tile)
        part = jnp.dot(held[i], grad_t[...], preferred_element_type=F32)
        s = part * jnp.concatenate([gains[at, :], gains[at, :]], axis=1)
        scaled[at, :] = s
        going.append(pltpu.make_async_copy(scaled.at[at, :], out.at[at, :], sems.at[pieces + i]))
        going[i].start()
        total = total + jnp.sum(s, axis=0, keepdims=True)
        along = along + jnp.sum(s * unit_of(xt[at, :], mean, scale), axis=0, keepdims=True)
    rest = jnp.zeros((BLK - 4, ROWS), F32)
    stats[...] = jnp.concatenate([total / DV, along / DV, mean, scale, rest], axis=0)
    size = first.shape[0] - HEAD
    at = pl.ds(pl.multiple_of(which[0] * size, BLK), size)
    store_coded(first, share_of(scaled[at, :], xt[at, :], stats[...]))
    for copy in going:
        copy.wait()


def scaled_of(own, starts, owners, which, back, w, xt, gains, inv, ranks, slots, parts):
    width = w.shape[1]
    size = DV // parts
    pieces = 5
    vmem = pl.BlockSpec(memory_space=pltpu.VMEM)
    return pl.pallas_call(
        functools.partial(scaled_kernel, ranks, slots, starts.shape[0]),
        in_specs=[smem()] * 4 + [vmem, pl.BlockSpec(memory_space=pl.ANY), vmem, vmem, vmem],
        out_specs=(pl.BlockSpec(memory_space=pltpu.HBM), vmem, vmem),
        out_shape=(
            pltpu.HBM((DV, ROWS), F32),
            struct((BLK, ROWS), F32),
            struct((HEAD + size, ROWS), I16),
        ),
        scratch_shapes=[
            pltpu.VMEM((ROWS, width), BF16),
            pltpu.VMEM((width, ROWS), BF16),
            pltpu.VMEM((DV, ROWS), F32),
            pltpu.VMEM((pieces, DV // pieces, width), BF16),
            pltpu.SemaphoreType.DMA((2 * pieces,)),
        ],
        compiler_params=params(57),
        cost_estimate=cost(2 * ROWS * DV * width, 2 * DV * width + 12 * ROWS * DV),
        name="scaled",
    )(own, starts, owners, which, back, w, xt, gains, inv)


def chunks_kernel(coded_count, which, scaled, xt, stats, *outs):
    size = outs[-1].shape[0]
    for k, out in enumerate(outs):
        at = pl.ds(pl.multiple_of(which[k] * size, BLK), size)
        share = share_of(scaled[at, :], xt[at, :], stats[...])
        if k < coded_count:
            store_coded(out, share)
        else:
            out[...] = share


def chunks_of(which, coded_count, scaled, xt, stats, parts):
    vmem = pl.BlockSpec(memory_space=pltpu.VMEM)
    count = which.shape[0]
    size = DV // parts
    kinds = [struct((HEAD + size, ROWS), I16)] * coded_count
    kinds += [struct((size, ROWS), F32)] * (count - coded_count)
    return pl.pallas_call(
        functools.partial(chunks_kernel, coded_count),
        in_specs=[smem(), vmem, vmem, vmem],
        out_specs=[vmem] * count,
        out_shape=kinds,
        compiler_params=params(),
        cost_estimate=cost(4 * count * size * ROWS, 12 * count * size * ROWS),
        name="chunks",
    )(which, scaled, xt, stats)


def relay_kernel(share, came, valid, out):
    store_coded(out, share[...] + jnp.where(valid[0] > 0, decoded(came), 0.0))


def finish_four_kernel(share, a, b, c, n, middle, out):
    total = share[...] + decoded(b)
    total = total + jnp.where(middle[0] > 0, decoded(c) + decoded(n), decoded(a))
    out[...] = total.astype(BF16)


def finish_kernel(share, one, other, valid, out):
    out[...] = (share[...] + decoded(one) + decoded(other)).astype(BF16)


def plain_call(kernel, name, kind, share, *extras):
    vmem = pl.BlockSpec(memory_space=pltpu.VMEM)
    size, lanes = share.shape
    return pl.pallas_call(
        kernel,
        in_specs=[vmem] * len(extras) + [smem()],
        out_specs=vmem,
        out_shape=struct((size if kind == BF16 else HEAD + size, lanes), kind),
        compiler_params=params(),
        cost_estimate=cost(20 * size * lanes, 8 * size * lanes),
        name=name,
    )(share, *extras)


relay = functools.partial(plain_call, relay_kernel, "relay", I16)
finish = functools.partial(plain_call, finish_kernel, "finish", BF16)
finish_four = functools.partial(plain_call, finish_four_kernel, "finish", BF16)


def chunk_order(place, parts):
    last = parts - 1
    if parts == 4:
        low = place < 2
        order = [
            jnp.where(place % 2 == 0, 3, 0),
            jnp.where(low, 2, 1),
            jnp.where(low, 1, 2),
            (place + 2) % 4,
            place,
        ]
    else:
        order = [jnp.full_like(place, last), jnp.zeros_like(place)]
        for s in range(1, last):
            order += [jnp.minimum(last - s + place, last), jnp.maximum(place - last + s, 0)]
        order += [place]
    return jnp.stack(order)


def scatter_sum(first, order, scaled, xt, stats, place, parts):
    last = parts - 1
    if parts == 4:
        outer, inner = [(0, 1), (1, 0), (2, 3), (3, 2)], [(0, 0), (1, 2), (2, 1), (3, 3)]
        across = [(0, 2), (1, 3), (2, 0), (3, 1)]
        middle = ((place == 1) | (place == 2)).astype(I32).reshape(1)
        a = lax.ppermute(first, "mp", outer)
        for_n, for_c, for_b, own = chunks_of(order[1:], 2, scaled, xt, stats, parts)
        n = lax.ppermute(for_n, "mp", inner)
        for_c, a, n_done = lax.optimization_barrier((for_c, a, for_n))
        c = lax.ppermute(for_c, "mp", outer)
        b = lax.ppermute(relay(for_b, a, middle), "mp", across)
        return finish_four(own, a, b, c, n, middle)
    held = chunks_of(order[1:], 1, scaled, xt, stats, parts)
    up, down = first, held[0]
    always = jnp.ones((1,), I32)
    for s in range(1, parts):
        up = lax.ppermute(up, "mp", [(z, z + 1) for z in range(s)])
        down = lax.ppermute(down, "mp", [(last - z, last - z - 1) for z in range(s)])
        if s < last:
            up, down = relay(held[2 * s - 1], up, always), relay(held[2 * s], down, always)
    return finish(held[-1], up, down, always)


def summed(values, parts):
    if parts & (parts - 1):
        return lax.psum(values, "mp")
    hop = 1
    while hop < parts:
        values = values + lax.ppermute(values, "mp", [(i, i ^ hop) for i in range(parts)])
        hop *= 2
    return values


def exchange(rows, ranks):
    shape = rows.shape
    split = rows.reshape(ranks, shape[0] // ranks, shape[1])
    return lax.all_to_all(split, "seq", split_axis=0, concat_axis=0, tiled=True).reshape(shape)


def body(
    vit_hidden,
    vit_gain,
    vit_bias,
    proj_weight,
    text_emb,
    llm_gain,
    cotangent,
    tile_start,
    tile_owner,
):
    ranks = lax.axis_size("seq")
    parts = lax.axis_size("mp")
    own_index = lax.axis_index("seq")
    place = lax.axis_index("mp")
    slots = -(-TILE_BLOCKS // ranks)
    width = proj_weight.shape[1]
    local_blocks = text_emb.shape[0] // BLK
    own = own_index.reshape(1)
    gain = llm_gain.reshape(1, width)

    sent = embed(own, tile_start, tile_owner, vit_hidden, vit_gain, vit_bias, proj_weight, ranks, slots)
    came = exchange(sent, ranks)

    global_block = (jnp.arange(local_blocks, dtype=I32) * ranks + own_index)[:, None]
    offset = global_block - tile_start[None, :]
    covered = (offset >= 0) & (offset < TILE_BLOCKS)
    slot_of = jnp.sum(
        jnp.where(covered, tile_owner[None, :] * slots + offset // ranks + 1, 0), axis=1
    ) - 1
    owners = jnp.arange(ranks, dtype=I32)[:, None]
    start_of = jnp.sum(jnp.where(tile_owner[None, :] == owners, tile_start[None, :], 0), axis=1)
    tile_block = (own_index - start_of[:, None]) % ranks + (
        jnp.arange(slots, dtype=I32)[None, :] * ranks
    )
    local_of = jnp.minimum((start_of[:, None] + tile_block) // ranks, local_blocks - 1)
    order = chunk_order(place, parts)
    local_of, slot_of, order = lax.optimization_barrier((local_of, slot_of, order))
    cot_blocks = cotangent.reshape(local_blocks, BLK, width)
    cot_image = jnp.take(cot_blocks, local_of.reshape(-1), axis=0, mode="clip")
    cot_image = cot_image.reshape(-1, width)

    text_part = text_sums(text_emb, cotangent, gain)

    sums = summed(image_sums(came, cot_image, gain, text_part), parts)
    back = exchange(image_grad(came, cot_image, gain, sums), ranks)
    normed, grad_text, after = outputs(slot_of, came, text_emb, cotangent, gain, sums)

    xt, gains, row_stats = turned_of(vit_hidden, vit_gain, after)
    scaled, stats, first = scaled_of(
        own, tile_start, tile_owner, order[:1], back, proj_weight, xt, gains, row_stats,
        ranks, slots, parts
    )
    grad_vit = scatter_sum(first, order, scaled, xt, stats, place, parts)
    return (normed, grad_text, grad_vit.T)


def solution(mesh):
    in_specs = (
        P("seq", None),
        P(),
        P(),
        P(None, "mp"),
        P("seq", "mp"),
        P("mp"),
        P("seq", "mp"),
        P(),
        P(),
    )
    out_specs = (P("seq", "mp"), P("seq", "mp"), P("seq", "mp"))
    return jax.shard_map(body, mesh=mesh, in_specs=in_specs, out_specs=out_specs, check_vma=False)
```
